512 devices in a mesh: segment: 64 (over x, z), node: 8 (over y, core).
Axes of the slice: x: 4, y: 4, z: 16, core: 2. Of those that a mesh axis runs over, the one named last changes fastest.
Arguments:
- node_feats: bfloat16 [4, 4, 1024, 512], P(None, None, 'node'), may hold values from -6 to 6
- self_tiles: bfloat16 [4, 4, 1024, 128], P(None, None, 'node'), may hold values from 0 to 0.18, as said below
- cross_tiles: bfloat16 [4, 4, 1024, 128], P(None, None, 'node'), may hold values from 0 to 0.18, as said below
- cross_live: int32 [4, 4, 8], P(None, None, 'node'), may hold values from 0 to 1
- w_self: bfloat16 [64, 512, 512], P('segment'), may hold values from -0.125 to 0.125
- w_nbr: bfloat16 [64, 512, 512], P('segment'), may hold values from -0.125 to 0.125
- w_out: bfloat16 [64, 512, 512], P('segment'), may hold values from -0.25 to 0.25
- norm_gain: float32 [64, 512], P('segment'), may hold values from 0.25 to 1.75
Outputs:
- saved_acts: bfloat16 [64, 4, 1024, 512], P('segment', None, 'node')
The draws below stay inside these ranges and needn't reach their ends.
Inputs may be any that keep to these rules, and one draw needn't show every extreme that they name: `self_tiles`: edge weights; zero where a node pair has no edge. `cross_tiles`: edge weights; zero where a node pair has no edge.
All inputs are finite; a program needn't handle non-finite values.
Results may differ from the reference program's by a relative error of at most 0.018.
Values may be sent and summed in bfloat16 or wider, within the bound.
No kernel may reach another device: no remote copies, remote signals or barrier semaphores. Data moves between devices by JAX's collectives and lax.ppermute only.
A program may use at most 64 MiB of HBM per device.

```python
import jax
import jax.numpy as jnp
from jax import lax

D = 512
TILE = 128
SECTIONS = 16
MB_DEV = 4
MEMBERS = 4
NODES = 1024
N_SEGMENT = 64
N_NODE = 8


def tile_values(key):
    shape = (N_SEGMENT // SECTIONS, MB_DEV, TILE * N_NODE, TILE)
    mask_key, value_key = jax.random.split(key)
    present = jax.random.bernoulli(mask_key, 0.35, shape).astype(jnp.float32)
    values = jax.random.uniform(value_key, shape, jnp.float32, 0.5, 1.5)
    return present * values * 0.1


def draw_self_tiles(key, part):
    return tile_values(jax.random.fold_in(key, 11)).astype(jnp.bfloat16)


def draw_cross_tiles(key, part):
    return tile_values(jax.random.fold_in(key, 23)).astype(jnp.bfloat16)


def touch_ends(entries, key, low, largest):
    place = [jax.random.randint(jax.random.fold_in(key, axis), (), 0, length) for axis, length in enumerate(entries.shape)]
    longest = entries.shape.index(max(entries.shape))
    neighbour = place[:longest] + [(place[longest] + 1) % entries.shape[longest]] + place[longest + 1:]
    return entries.at[tuple(place)].set(low).at[tuple(neighbour)].set(largest)


def block_levels(own_key, extent, shards, least, largest):
    gain, own = 1.0, jax.random.fold_in(own_key, 6)
    for dim, parts in shards:
        heights = jnp.exp(jax.random.uniform(jax.random.fold_in(own, dim), (parts,), jnp.float32, least / len(shards), largest / len(shards)))
        gain = gain * jnp.repeat(heights, extent[dim] // parts).reshape([-1 if axis == dim else 1 for axis in range(len(extent))])
    return gain


def centred(key, extent, width, reach, pieces=(), held_as=jnp.bfloat16):
    values = jax.random.normal(key, extent, jnp.float32) * width
    if len(pieces) > 0:
        values = block_levels(key, extent, pieces, -0.22, 0.18) * values
    return jnp.clip(values, min=-reach, max=reach).astype(held_as)


def setup_inputs(seed: int = 0) -> dict:
    keys = jax.random.split(jax.random.key(seed), 9)
    node_feats = centred(keys[0], (MEMBERS, MB_DEV, NODES, D), 1.0, 6.0, ((2, 8),))
    self_tiles = draw_self_tiles(jax.random.fold_in(keys[8], 71), 0)
    cross_tiles = draw_cross_tiles(jax.random.fold_in(keys[8], 71), 0)
    cross_live = touch_ends(jax.random.randint(keys[3], (MEMBERS, MB_DEV, N_NODE), 0, 2), jax.random.fold_in(keys[3], 1), 0, 1).astype(jnp.int32)
    w_self = centred(keys[4], (N_SEGMENT, D, D), (4 * D) ** -0.5, 0.125, ((0, 64),))
    w_nbr = centred(keys[5], (N_SEGMENT, D, D), (4 * D) ** -0.5, 0.125, ((0, 64),))
    w_out = centred(keys[6], (N_SEGMENT, D, D), D ** -0.5, 0.25, ((0, 64),))
    norm_gain = jnp.clip(1.0 + 0.15 * jax.random.normal(keys[7], (N_SEGMENT, D), jnp.float32), 0.25, 1.75)
    return dict(node_feats=node_feats, self_tiles=self_tiles, cross_tiles=cross_tiles, cross_live=cross_live, w_self=w_self, w_nbr=w_nbr, w_out=w_out, norm_gain=norm_gain)


def apply_layer(trunk, weight_self, weight_nbr, weight_out, gain_row, tile_self, tile_cross, live_flags):
    trunk_bf = trunk.astype(jnp.bfloat16)
    blocks = trunk_bf.reshape(N_NODE, TILE, D).astype(jnp.float32)
    self_blocks = tile_self.reshape(N_NODE, TILE, TILE).astype(jnp.float32)
    cross_blocks = tile_cross.reshape(N_NODE, TILE, TILE).astype(jnp.float32)
    own_sum = jnp.einsum('kds,ksf->kdf', self_blocks, blocks)
    sent = jnp.einsum('kds,ksf->kdf', cross_blocks, blocks)
    sent = sent * live_flags.astype(jnp.float32)[:, None, None]
    agg = (own_sum + jnp.roll(sent, 1, axis=0)).reshape(NODES, D).astype(jnp.bfloat16)
    pre = jnp.dot(trunk_bf, weight_self, preferred_element_type=jnp.float32)
    pre = pre + jnp.dot(agg, weight_nbr, preferred_element_type=jnp.float32)
    hidden = jax.nn.silu(pre).astype(jnp.bfloat16)
    value = trunk + jnp.dot(hidden, weight_out, preferred_element_type=jnp.float32)
    scale = lax.rsqrt(lax.optimization_barrier(jnp.mean(value * value, axis=-1, keepdims=True)) + 1e-06)
    return value * scale * gain_row

def reference(node_feats, self_tiles, cross_tiles, cross_live, w_self, w_nbr, w_out, norm_gain):
    members = N_SEGMENT // SECTIONS
    collected = []
    for member in range(members):
        params = (w_self.reshape(SECTIONS, members, D, D)[:, member], w_nbr.reshape(SECTIONS, members, D, D)[:, member], w_out.reshape(SECTIONS, members, D, D)[:, member], norm_gain.reshape(SECTIONS, members, D)[:, member])
        tiles_self = self_tiles[member]
        tiles_cross = cross_tiles[member]
        live_all = cross_live[member]

        def one_layer(trunk, layer_params):
            weight_self, weight_nbr, weight_out, gain_row = layer_params
            mapped = jax.vmap(apply_layer, in_axes=(0, None, None, None, None, 0, 0, 0))
            updated = mapped(trunk, weight_self, weight_nbr, weight_out, gain_row, tiles_self, tiles_cross, live_all)
            return (updated, updated.astype(jnp.bfloat16))
        start = node_feats[member].astype(jnp.float32)
        _, saved = lax.scan(one_layer, start, params)
        collected.append(saved)
    stacked = jnp.stack(collected, axis=1)
    return stacked.reshape(N_SEGMENT, MB_DEV, NODES, D)
```

```python
import functools

import jax
import jax.numpy as jnp
from jax import lax
from jax.experimental import pallas as pl
from jax.experimental.pallas import tpu as pltpu
from jax.sharding import PartitionSpec as P

BF = jnp.bfloat16
F32 = jnp.float32
D = 512
TILE = 128
HALF = TILE // 2
BLOCKS = 8
CHUNK = 2
MEMBERS = 4
AXES = ("segment", "node")
GAIN_ROWS = 16

STAGES = (
    (0, ((0,), (1,), (2, 3))),
    (1, ((4, 5, 6, 7),)),
    (2, ((8, 9, 10, 11),)),
    (3, ((12, 13), (14,), (15,))),
)


def layers_of(stage):
    return [layer for group in stage[1] for layer in group]


SLOTS = max(len(layers_of(stage)) for stage in STAGES)


def device(x, a, m, y, c):
    return (x * 16 + a * 4 + m) * BLOCKS + y * 2 + c


def chain_a(m):
    return m


def pairs_over(fn):
    return [fn(m, y) for m in range(MEMBERS) for y in range(4)]


def weight_route(slot):
    route = []
    for place, _groups in STAGES:
        layers = layers_of((place, _groups))
        if slot < len(layers):
            lx, la = divmod(layers[slot], 4)
            route += pairs_over(
                lambda m, y: (device(lx, la, m, y, 0), device(place, chain_a(m), m, y, 0))
            )
    return route


def result_route(slot, half):
    route = []
    for place, _groups in STAGES:
        layers = layers_of((place, _groups))
        if slot < len(layers):
            lx, la = divmod(layers[slot], 4)
            route += pairs_over(
                lambda m, y: (device(place, chain_a(m), m, y, 0), device(lx, la, m, y, half))
            )
    return route


def stage_route(here, there):
    return pairs_over(
        lambda m, y: (device(here, chain_a(m), m, y, 0), device(there, chain_a(m), m, y, 0))
    )


def layers_kernel(count, aliased, kind_in, kind_out, *refs):
    active, state, gathered = refs[:3]
    weights = refs[3 : 3 + count]
    at = 3 + count + 2 * aliased
    outs = [refs[at + 2 * i : at + 2 * i + 2] for i in range(count)]
    at += 2 * count
    state_out = None
    if kind_out:
        state_out = refs[at]
        at += 1
    held, tiles, arrived, nodes, trunk, in_sems, out_sems = refs[at:]

    @pl.when(active[0] == 1)
    def _():
        weight_copies = [
            pltpu.make_async_copy(weights[i], held.at[i], in_sems.at[i]) for i in range(count)
        ]
        tile_copy = pltpu.make_async_copy(
            gathered.at[:, :, pl.ds(D, 2 * TILE)], tiles, in_sems.at[count]
        )
        source = gathered.at[:, :, pl.ds(0, D)] if kind_in == "gathered" else state
        state_copy = pltpu.make_async_copy(
            source, trunk if kind_in == "f32" else arrived, in_sems.at[count + 1]
        )
        state_copy.start()
        tile_copy.start()
        for copy in weight_copies:
            copy.start()
        state_copy.wait()
        if kind_in == "f32":
            start = trunk[...].astype(BF)
        else:
            start = arrived[...]
            trunk[...] = start.astype(F32)
        nodes[0, 1 : BLOCKS + 1] = start
        nodes[0, 0] = start[BLOCKS - 1]
        tile_copy.wait()
        earlier = []
        for i in range(count):
            now = i % 2
            later = 1 - now
            weight_copies[i].wait()
            gain = held[i, 3 * D : 3 * D + GAIN_ROWS, :].astype(F32)
            gain = gain[0:1] + gain[1:2] + gain[2:3]
            for first in range(0, BLOCKS, CHUNK):
                sums = []
                for k in range(first, first + CHUNK):
                    both = jnp.concatenate(
                        [tiles[(k - 1) % BLOCKS, :, TILE:], tiles[k, :, :TILE]], axis=1
                    )
                    pair = nodes[now, k : k + 2].reshape(2 * TILE, D)
                    sums.append(jnp.dot(both, pair, preferred_element_type=F32).astype(BF))
                agg = jnp.concatenate(sums, axis=0)
                own = nodes[now, 1 + first : 1 + first + CHUNK].reshape(CHUNK * TILE, D)
                pre = jnp.dot(own, held[i, 0:D, :], preferred_element_type=F32)
                pre = pre + jnp.dot(agg, held[i, D : 2 * D, :], preferred_element_type=F32)
                hidden = jax.nn.silu(pre).astype(BF)
                value = trunk[first : first + CHUNK].reshape(CHUNK * TILE, D) + jnp.dot(
                    hidden, held[i, 2 * D : 3 * D, :], preferred_element_type=F32
                )
                scale = lax.rsqrt(jnp.mean(value * value, axis=-1, keepdims=True) + 1e-06)
                updated = (value * scale * gain).reshape(CHUNK, TILE, D)
                trunk[first : first + CHUNK] = updated
                new_nodes = updated.astype(BF)
                nodes[later, 1 + first : 1 + first + CHUNK] = new_nodes
                if first + CHUNK == BLOCKS:
                    nodes[later, 0] = new_nodes[CHUNK - 1]
            copies = [
                pltpu.make_async_copy(
                    nodes.at[later, pl.ds(1, BLOCKS), pl.ds(h * HALF, HALF)],
                    outs[i][h],
                    out_sems.at[later, h],
                )
                for h in range(2)
            ]
            if i == count - 1 and kind_out == "bf16":
                copies.append(
                    pltpu.make_async_copy(
                        nodes.at[later, pl.ds(1, BLOCKS)], state_out, out_sems.at[later, 2]
                    )
                )
            if i == count - 1 and kind_out == "f32":
                copies.append(pltpu.make_async_copy(trunk, state_out, out_sems.at[later, 2]))
            for copy in copies:
                copy.start()
            for copy in earlier:
                copy.wait()
            earlier = copies
        for copy in earlier:
            copy.wait()


def run_layers(active, state, gathered, weights, outs, kind_in, kind_out):
    count = len(weights)
    aliased = len(outs) // 2
    shapes = [jax.ShapeDtypeStruct((BLOCKS, HALF, D), BF)] * (2 * count)
    if kind_out:
        shapes.append(
            jax.ShapeDtypeStruct((BLOCKS, TILE, D), BF if kind_out == "bf16" else F32)
        )
    where = pl.BlockSpec(memory_space=pl.ANY)
    results = pl.pallas_call(
        functools.partial(layers_kernel, count, aliased, kind_in, kind_out),
        out_shape=shapes,
        in_specs=[pl.BlockSpec(memory_space=pltpu.SMEM)] + [where] * (2 + count + 2 * aliased),
        out_specs=[where] * len(shapes),
        input_output_aliases={3 + count + i: i for i in range(2 * aliased)},
        scratch_shapes=[
            pltpu.VMEM((count, 3 * D + GAIN_ROWS, D), BF),
            pltpu.VMEM((BLOCKS, TILE, 2 * TILE), BF),
            pltpu.VMEM((BLOCKS, TILE, D), BF),
            pltpu.VMEM((2, BLOCKS + 1, TILE, D), BF),
            pltpu.VMEM((BLOCKS, TILE, D), F32),
            pltpu.SemaphoreType.DMA((count + 2,)),
            pltpu.SemaphoreType.DMA((2, 3)),
        ],
        compiler_params=pltpu.CompilerParams(vmem_limit_bytes=40 << 20),
        cost_estimate=pl.CostEstimate(
            flops=count * 1_880_000_000, bytes_accessed=count * 4_000_000, transcendentals=0
        ),
    )(active, state, gathered, *weights, *outs)
    return results[: 2 * count], (results[2 * count] if kind_out else None)


def gain_as_rows(gain):
    high = lax.reduce_precision(gain, 8, 7)
    middle = lax.reduce_precision(gain - high, 8, 7)
    low = lax.reduce_precision(gain - high - middle, 8, 7)
    rows = jnp.stack([high, middle, low]).astype(BF)
    return jnp.pad(rows, ((0, GAIN_ROWS - 3), (0, 0)))


def on_device(node_feats, self_tiles, cross_tiles, cross_live, w_self, w_nbr, w_out, norm_gain):
    segment = lax.axis_index("segment")
    node = lax.axis_index("node")
    x, z = segment // 16, segment % 16
    a, member = z // 4, z % 4
    core = node % 2

    packed = jnp.concatenate([w_self[0], w_nbr[0], w_out[0], gain_as_rows(norm_gain[0])], axis=0)
    weights = [lax.ppermute(packed, AXES, weight_route(slot)) for slot in range(SLOTS)]

    live = cross_live[member].astype(BF)[:, :, None]
    sent = jnp.concatenate(
        [node_feats[member], self_tiles[member], cross_tiles[member] * live], axis=-1
    )
    sent = jnp.broadcast_to(sent[:, None], (4, 2) + sent.shape[1:]).reshape((8,) + sent.shape[1:])
    gathered = lax.all_to_all(sent, "node", 0, 0, tiled=True)

    outs = [None] * SLOTS
    state = gathered
    on_chain = jnp.logical_and(a == member, core == 0)
    for t, (place, groups) in enumerate(STAGES):
        active = jnp.logical_and(on_chain, x == place).astype(jnp.int32).reshape(1)
        slot = 0
        kind_in = "gathered" if t == 0 else "bf16"
        for g, group in enumerate(groups):
            slots = range(slot, slot + len(group))
            last = g == len(groups) - 1
            kind_out = "f32" if not last else ("bf16" if t < len(STAGES) - 1 else None)
            old = [h for s in slots if outs[s] is not None for h in outs[s]]
            new, state = run_layers(
                active, state, gathered, [weights[s] for s in slots], old, kind_in, kind_out
            )
            for i, s in enumerate(slots):
                outs[s] = new[2 * i : 2 * i + 2]
            kind_in = "f32"
            slot += len(group)
        if t < len(STAGES) - 1:
            state = lax.ppermute(state, AXES, stage_route(place, STAGES[t + 1][0]))

    slot_of = [0] * 16
    for stage in STAGES:
        for s, layer in enumerate(layers_of(stage)):
            slot_of[layer] = s
    chosen = jnp.asarray(slot_of, jnp.int32)[x * 4 + a]
    home = None
    for s in range(SLOTS):
        r = lax.ppermute(outs[s][0], AXES, result_route(s, 0))
        r1 = lax.ppermute(outs[s][1], AXES, result_route(s, 1))
        r = jnp.where(core == 0, r, r1)
        home = r if home is None else jnp.where(chosen == s, r, home)
    spread = lax.all_to_all(home, "node", 0, 0, tiled=True)
    return spread.reshape(1, 4, TILE, D)


def solution(mesh):
    return jax.shard_map(
        on_device,
        mesh=mesh,
        in_specs=(
            P(None, None, "node", None),
            P(None, None, "node", None),
            P(None, None, "node", None),
            P(None, None, "node"),
            P("segment", None, None),
            P("segment", None, None),
            P("segment", None, None),
            P("segment", None),
        ),
        out_specs=P("segment", None, "node", None),
        check_vma=False,
    )
```

```python
import functools

import jax
import jax.numpy as jnp
from jax import lax
from jax.experimental import pallas as pl
from jax.experimental.pallas import tpu as pltpu
from jax.sharding import PartitionSpec as P

BF = jnp.bfloat16
F32 = jnp.float32
D = 512
TILE = 128
HALF = TILE // 2
BLOCKS = 8
CHUNK = 2
MEMBERS = 4
AXES = ("segment", "node")
GAIN_ROWS = 16

STAGES = (
    (0, ((0,), (1,), (2, 3), (4, 5, 6, 7))),
    (3, ((8, 9, 10, 11), (12, 13), (14, 15))),
)


def layers_of(stage):
    return [layer for group in stage[1] for layer in group]


SLOTS = max(len(layers_of(stage)) for stage in STAGES)


def device(x, a, m, y, c):
    return (x * 16 + a * 4 + m) * BLOCKS + y * 2 + c


def chain_a(m):
    return m


def pairs_over(fn):
    pairs = [fn(m, y) for m in range(MEMBERS) for y in range(4)]
    return [(source, target) for source, target in pairs if source != target]


def weight_route(slot):
    route = []
    for place, _groups in STAGES:
        layers = layers_of((place, _groups))
        if slot < len(layers):
            lx, la = divmod(layers[slot], 4)
            route += pairs_over(
                lambda m, y: (device(lx, la, m, y, 0), device(place, chain_a(m), m, y, 0))
            )
    return route


def result_route(slot, half):
    route = []
    for place, _groups in STAGES:
        layers = layers_of((place, _groups))
        if slot < len(layers):
            lx, la = divmod(layers[slot], 4)
            route += pairs_over(
                lambda m, y: (device(place, chain_a(m), m, y, 0), device(lx, la, m, y, half))
            )
    return route


def stage_route(here, there):
    return pairs_over(
        lambda m, y: (device(here, chain_a(m), m, y, 0), device(there, chain_a(m), m, y, 0))
    )


def layers_kernel(count, aliased, kind_in, kind_out, *refs):
    flags, state, gathered, packed = refs[:4]
    weights = refs[4 : 4 + count]
    at = 4 + count + 2 * aliased
    outs = [refs[at + 2 * i : at + 2 * i + 2] for i in range(count)]
    at += 2 * count
    state_out = None
    if kind_out:
        state_out = refs[at]
        at += 1
    held, tiles, arrived, nodes, trunk, in_sems, out_sems = refs[at:]

    @pl.when(flags[0] == 1)
    def _():
        weight_copies = [
            pltpu.make_async_copy(weights[i], held.at[i], in_sems.at[i]) for i in range(count)
        ]
        tile_copy = pltpu.make_async_copy(
            gathered.at[:, :, pl.ds(D, 2 * TILE)], tiles, in_sems.at[count]
        )
        source = gathered.at[:, :, pl.ds(0, D)] if kind_in == "gathered" else state
        state_copy = pltpu.make_async_copy(
            source, trunk if kind_in == "f32" else arrived, in_sems.at[count + 1]
        )
        state_copy.start()
        tile_copy.start()
        for i in range(count):
            own = pltpu.make_async_copy(packed, held.at[i], in_sems.at[i])
            pl.when(flags[1 + i] == 1)(own.start)
            pl.when(flags[1 + i] == 0)(weight_copies[i].start)
        state_copy.wait()
        if kind_in == "f32":
            start = trunk[...].astype(BF)
        else:
            start = arrived[...]
            trunk[...] = start.astype(F32)
        nodes[0, 1 : BLOCKS + 1] = start
        nodes[0, 0] = start[BLOCKS - 1]
        tile_copy.wait()
        earlier = []
        for i in range(count):
            now = i % 2
            later = 1 - now
            weight_copies[i].wait()
            gain = held[i, 3 * D : 3 * D + GAIN_ROWS, :].astype(F32)
            gain = gain[0:1] + gain[1:2] + gain[2:3]
            for first in range(0, BLOCKS, CHUNK):
                sums = []
                for k in range(first, first + CHUNK):
                    both = jnp.concatenate(
                        [tiles[(k - 1) % BLOCKS, :, TILE:], tiles[k, :, :TILE]], axis=1
                    )
                    pair = nodes[now, k : k + 2].reshape(2 * TILE, D)
                    sums.append(jnp.dot(both, pair, preferred_element_type=F32).astype(BF))
                agg = jnp.concatenate(sums, axis=0)
                own = nodes[now, 1 + first : 1 + first + CHUNK].reshape(CHUNK * TILE, D)
                pre = jnp.dot(own, held[i, 0:D, :], preferred_element_type=F32)
                pre = pre + jnp.dot(agg, held[i, D : 2 * D, :], preferred_element_type=F32)
                hidden = jax.nn.silu(pre).astype(BF)
                value = trunk[first : first + CHUNK].reshape(CHUNK * TILE, D) + jnp.dot(
                    hidden, held[i, 2 * D : 3 * D, :], preferred_element_type=F32
                )
                scale = lax.rsqrt(jnp.mean(value * value, axis=-1, keepdims=True) + 1e-06)
                updated = (value * scale * gain).reshape(CHUNK, TILE, D)
                trunk[first : first + CHUNK] = updated
                new_nodes = updated.astype(BF)
                nodes[later, 1 + first : 1 + first + CHUNK] = new_nodes
                if first + CHUNK == BLOCKS:
                    nodes[later, 0] = new_nodes[CHUNK - 1]
            copies = [
                pltpu.make_async_copy(
                    nodes.at[later, pl.ds(1, BLOCKS), pl.ds(h * HALF, HALF)],
                    outs[i][h],
                    out_sems.at[later, h],
                )
                for h in range(2)
            ]
            if i == count - 1 and kind_out == "bf16":
                copies.append(
                    pltpu.make_async_copy(
                        nodes.at[later, pl.ds(1, BLOCKS)], state_out, out_sems.at[later, 2]
                    )
                )
            if i == count - 1 and kind_out == "f32":
                copies.append(pltpu.make_async_copy(trunk, state_out, out_sems.at[later, 2]))
            for copy in copies:
                copy.start()
            for copy in earlier:
                copy.wait()
            earlier = copies
        for copy in earlier:
            copy.wait()


def run_layers(flags, state, gathered, packed, weights, outs, kind_in, kind_out):
    count = len(weights)
    aliased = len(outs) // 2
    shapes = [jax.ShapeDtypeStruct((BLOCKS, HALF, D), BF)] * (2 * count)
    if kind_out:
        shapes.append(
            jax.ShapeDtypeStruct((BLOCKS, TILE, D), BF if kind_out == "bf16" else F32)
        )
    where = pl.BlockSpec(memory_space=pltpu.HBM)
    results = pl.pallas_call(
        functools.partial(layers_kernel, count, aliased, kind_in, kind_out),
        out_shape=shapes,
        in_specs=[pl.BlockSpec(memory_space=pltpu.SMEM)] + [where] * (3 + count + 2 * aliased),
        out_specs=[where] * len(shapes),
        input_output_aliases={4 + count + i: i for i in range(2 * aliased)},
        scratch_shapes=[
            pltpu.VMEM((count, 3 * D + GAIN_ROWS, D), BF),
            pltpu.VMEM((BLOCKS, TILE, 2 * TILE), BF),
            pltpu.VMEM((BLOCKS, TILE, D), BF),
            pltpu.VMEM((2, BLOCKS + 1, TILE, D), BF),
            pltpu.VMEM((BLOCKS, TILE, D), F32),
            pltpu.SemaphoreType.DMA((count + 2,)),
            pltpu.SemaphoreType.DMA((2, 3)),
        ],
        compiler_params=pltpu.CompilerParams(vmem_limit_bytes=62 << 20),
        cost_estimate=pl.CostEstimate(
            flops=count * 1_880_000_000, bytes_accessed=count * 4_000_000, transcendentals=0
        ),
    )(flags, state, gathered, packed, *weights, *outs)
    return results[: 2 * count], (results[2 * count] if kind_out else None)


def pick_kernel(chosen, *refs):
    out = refs[-1]
    for i, source in enumerate(refs[:-1]):
        @pl.when(chosen[0] == i)
        def _():
            pltpu.sync_copy(source, out)


def pick(chosen, sources):
    return pl.pallas_call(
        pick_kernel,
        out_shape=jax.ShapeDtypeStruct(sources[0].shape, sources[0].dtype),
        in_specs=[pl.BlockSpec(memory_space=pltpu.SMEM)]
        + [pl.BlockSpec(memory_space=pltpu.HBM)] * len(sources),
        out_specs=pl.BlockSpec(memory_space=pltpu.VMEM),
    )(chosen, *sources)


def gain_as_rows(gain):
    high = lax.reduce_precision(gain, 8, 7)
    middle = lax.reduce_precision(gain - high, 8, 7)
    low = lax.reduce_precision(gain - high - middle, 8, 7)
    rows = jnp.stack([high, middle, low]).astype(BF)
    return jnp.pad(rows, ((0, GAIN_ROWS - 3), (0, 0)))


def on_device(node_feats, self_tiles, cross_tiles, cross_live, w_self, w_nbr, w_out, norm_gain):
    segment = lax.axis_index("segment")
    node = lax.axis_index("node")
    x, z = segment // 16, segment % 16
    a, member = z // 4, z % 4
    core = node % 2

    packed = jnp.concatenate([w_self[0], w_nbr[0], w_out[0], gain_as_rows(norm_gain[0])], axis=0)
    weights = [lax.ppermute(packed, AXES, weight_route(slot)) for slot in range(SLOTS)]

    live = cross_live[member].astype(BF)[:, :, None]
    sent = jnp.concatenate(
        [node_feats[member], self_tiles[member], cross_tiles[member] * live], axis=-1
    )
    sent = jnp.broadcast_to(sent[:, None], (4, 2) + sent.shape[1:]).reshape((8,) + sent.shape[1:])
    gathered = lax.all_to_all(sent, "node", 0, 0, tiled=True)

    outs = [None] * SLOTS
    state = gathered
    on_chain = jnp.logical_and(a == member, core == 0)
    for t, (place, groups) in enumerate(STAGES):
        active = jnp.logical_and(on_chain, x == place)
        slot = 0
        kind_in = "gathered" if t == 0 else "bf16"
        for g, group in enumerate(groups):
            slots = range(slot, slot + len(group))
            last = g == len(groups) - 1
            kind_out = "f32" if not last else ("bf16" if t < len(STAGES) - 1 else None)
            old = [h for s in slots if outs[s] is not None for h in outs[s]]
            local = [jnp.logical_and(x == layer // 4, a == layer % 4) for layer in group]
            flags = jnp.stack([active] + local).astype(jnp.int32)
            new, state = run_layers(
                flags, state, gathered, packed, [weights[s] for s in slots], old, kind_in, kind_out
            )
            for i, s in enumerate(slots):
                outs[s] = new[2 * i : 2 * i + 2]
            kind_in = "f32"
            slot += len(group)
        if t < len(STAGES) - 1:
            state = lax.ppermute(state, AXES, stage_route(place, STAGES[t + 1][0]))

    slot_of = [0] * 16
    place_of = [0] * 16
    for stage in STAGES:
        for s, layer in enumerate(layers_of(stage)):
            slot_of[layer] = s
            place_of[layer] = stage[0]
    layer = x * 4 + a
    stays = jnp.logical_and(on_chain, x == jnp.asarray(place_of, jnp.int32)[layer])
    chosen = jnp.asarray(slot_of, jnp.int32)[layer]
    chosen = jnp.where(stays, 2 * SLOTS + chosen, chosen * 2 + core)
    sources = [
        lax.ppermute(outs[s][h], AXES, result_route(s, h)) for s in range(SLOTS) for h in range(2)
    ]
    home = pick(chosen.reshape(1), sources + [out[0] for out in outs])
    spread = lax.all_to_all(home, "node", 0, 0, tiled=True)
    return spread.reshape(1, 4, TILE, D)


def solution(mesh):
    return jax.shard_map(
        on_device,
        mesh=mesh,
        in_specs=(
            P(None, None, "node", None),
            P(None, None, "node", None),
            P(None, None, "node", None),
            P(None, None, "node"),
            P("segment", None, None),
            P("segment", None, None),
            P("segment", None, None),
            P("segment", None),
        ),
        out_specs=P("segment", None, "node", None),
        check_vma=False,
    )
```

```python
import functools

import jax
import jax.numpy as jnp
import numpy as np
from jax import lax
from jax.experimental import pallas as pl
from jax.experimental.pallas import tpu as pltpu
from jax.sharding import PartitionSpec as P

BF = jnp.bfloat16
F32 = jnp.float32
D = 512
TILE = 128
BLOCKS = 8
CHUNK = 2
MEMBERS = 4
AXES = ("segment", "node")
GAIN_ROWS = 16

STAGES = (
    (((0, 0), (0, 1), (0, 2), (0, 3)), ((0, 1), (2, 3, 4))),
    (((1, 0), (1, 1), (1, 2), (1, 3)), ((5, 6, 7, 8, 9, 10),)),
    (((3, 0), (2, 2), (0, 3), (2, 3)), ((11, 12, 13), (14, 15))),
)


def layers_of(t):
    return [layer for group in STAGES[t][1] for layer in group]


SLOTS = max(len(layers_of(t)) for t in range(len(STAGES)))
DEVICES = 512


def device(x, a, m, y, c):
    return (x * 16 + a * 4 + m) * BLOCKS + y * 2 + c


def over_chains(fn):
    pairs = [fn(m, y) for m in range(MEMBERS) for y in range(4)]
    return [(source, target) for source, target in pairs if source != target]


def chain(t, m, y):
    x, a = STAGES[t][0][m]
    return device(x, a, m, y, 0)


def home_of(layer, m, y):
    return device(layer // 4, layer % 4, m, y, 0)


def weight_route(slot):
    route = []
    for t in range(len(STAGES)):
        if slot < len(layers_of(t)):
            layer = layers_of(t)[slot]
            route += over_chains(lambda m, y: (home_of(layer, m, y), chain(t, m, y)))
    return route


def result_route(slot, stages):
    route = []
    for t in stages:
        if slot < len(layers_of(t)):
            layer = layers_of(t)[slot]
            route += over_chains(lambda m, y: (chain(t, m, y), home_of(layer, m, y)))
    return route


def stage_route(t):
    return over_chains(lambda m, y: (chain(t, m, y), chain(t + 1, m, y)))


STAGE_WIDTH = 1 + SLOTS
PICK_AT = len(STAGES) * STAGE_WIDTH


def flag_table():
    table = np.zeros((DEVICES, PICK_AT + 1), np.int32)
    for t in range(len(STAGES)):
        for m in range(MEMBERS):
            for y in range(4):
                at = chain(t, m, y)
                table[at, t * STAGE_WIDTH] = 1
                for slot, layer in enumerate(layers_of(t)):
                    home = home_of(layer, m, y)
                    table[at, t * STAGE_WIDTH + 1 + slot] = int(home == at)
                    table[home, PICK_AT] = slot + (SLOTS if home == at else 0)
    return table


def layers_kernel(t, first_slot, count, aliased, kind_in, *refs):
    flags, gathered, packed = refs[:3]
    at = 3
    states = refs[at : at + (0 if kind_in == "gathered" else 1)]
    at += len(states)
    weights = refs[at : at + count]
    at += count + aliased
    outs = refs[at : at + count]
    held, tiles, nodes, trunk, in_sems, out_sems = refs[at + count :]
    base = t * STAGE_WIDTH

    @pl.when(flags[base] == 1)
    def _():
        source = gathered.at[:, :, pl.ds(0, D)] if kind_in == "gathered" else states[0]
        state_copy = pltpu.make_async_copy(
            source, nodes.at[0, pl.ds(1, BLOCKS)], in_sems.at[count + 1]
        )
        tile_copy = pltpu.make_async_copy(
            gathered.at[:, :, pl.ds(D, 2 * TILE)], tiles, in_sems.at[count]
        )
        weight_copies = [
            pltpu.make_async_copy(weights[i], held.at[i], in_sems.at[i]) for i in range(count)
        ]
        state_copy.start()
        tile_copy.start()
        for i in range(count):
            own = pltpu.make_async_copy(packed, held.at[i], in_sems.at[i])
            mine = flags[base + 1 + first_slot + i]
            pl.when(mine == 1)(own.start)
            pl.when(mine == 0)(weight_copies[i].start)
        state_copy.wait()
        nodes[0, 0] = nodes[0, BLOCKS]
        tile_copy.wait()
        earlier = None
        for i in range(count):
            now = i % 2
            later = 1 - now
            weight_copies[i].wait()
            gain = held[i, 3 * D : 3 * D + GAIN_ROWS, :].astype(F32)
            gain = gain[0:1] + gain[1:2] + gain[2:3]
            for first in range(0, BLOCKS, CHUNK):
                sums = []
                for k in range(first, first + CHUNK):
                    both = jnp.concatenate(
                        [tiles[(k - 1) % BLOCKS, :, TILE:], tiles[k, :, :TILE]], axis=1
                    )
                    pair = nodes[now, k : k + 2].reshape(2 * TILE, D)
                    sums.append(jnp.dot(both, pair, preferred_element_type=F32).astype(BF))
                agg = jnp.concatenate(sums, axis=0)
                own = nodes[now, 1 + first : 1 + first + CHUNK].reshape(CHUNK * TILE, D)
                pre = jnp.dot(own, held[i, 0:D, :], preferred_element_type=F32)
                pre = pre + jnp.dot(agg, held[i, D : 2 * D, :], preferred_element_type=F32)
                hidden = jax.nn.silu(pre).astype(BF)
                if i == 0:
                    before = own.astype(F32)
                else:
                    before = trunk[first : first + CHUNK].reshape(CHUNK * TILE, D)
                value = before + jnp.dot(
                    hidden, held[i, 2 * D : 3 * D, :], preferred_element_type=F32
                )
                scale = lax.rsqrt(jnp.mean(value * value, axis=-1, keepdims=True) + 1e-06)
                updated = (value * scale * gain).reshape(CHUNK, TILE, D)
                if i < count - 1:
                    trunk[first : first + CHUNK] = updated
                new_nodes = updated.astype(BF)
                nodes[later, 1 + first : 1 + first + CHUNK] = new_nodes
                if first + CHUNK == BLOCKS and i < count - 1:
                    nodes[later, 0] = new_nodes[CHUNK - 1]
            copy = pltpu.make_async_copy(
                nodes.at[later, pl.ds(1, BLOCKS)], outs[i], out_sems.at[later]
            )
            copy.start()
            if earlier is not None:
                earlier.wait()
            earlier = copy
        earlier.wait()


def run_layers(t, first_slot, flags, gathered, packed, state, weights, outs):
    count = len(weights)
    kind_in = "gathered" if state is None else "bf16"
    states = [] if state is None else [state]
    where = pl.BlockSpec(memory_space=pltpu.HBM)
    n_in = 3 + len(states) + count
    return pl.pallas_call(
        functools.partial(layers_kernel, t, first_slot, count, len(outs), kind_in),
        out_shape=[jax.ShapeDtypeStruct((BLOCKS, TILE, D), BF)] * count,
        in_specs=[pl.BlockSpec(memory_space=pltpu.SMEM)] + [where] * (n_in - 1 + len(outs)),
        out_specs=[where] * count,
        input_output_aliases={n_in + i: i for i in range(len(outs))},
        scratch_shapes=[
            pltpu.VMEM((count, 3 * D + GAIN_ROWS, D), BF),
            pltpu.VMEM((BLOCKS, TILE, 2 * TILE), BF),
            pltpu.VMEM((2, BLOCKS + 1, TILE, D), BF),
            pltpu.VMEM((BLOCKS, TILE, D), F32),
            pltpu.SemaphoreType.DMA((count + 2,)),
            pltpu.SemaphoreType.DMA((2,)),
        ],
        compiler_params=pltpu.CompilerParams(vmem_limit_bytes=62 << 20),
        cost_estimate=pl.CostEstimate(
            flops=count * 1_880_000_000, bytes_accessed=count * 4_000_000, transcendentals=0
        ),
    )(flags, gathered, packed, *states, *weights, *outs)


def pick_kernel(flags, *refs):
    out = refs[-1]
    for i, source in enumerate(refs[:-1]):
        @pl.when(flags[PICK_AT] == i)
        def _():
            pltpu.sync_copy(source, out)


def pick(flags, sources):
    return pl.pallas_call(
        pick_kernel,
        out_shape=jax.ShapeDtypeStruct(sources[0].shape, sources[0].dtype),
        in_specs=[pl.BlockSpec(memory_space=pltpu.SMEM)]
        + [pl.BlockSpec(memory_space=pltpu.HBM)] * len(sources),
        out_specs=pl.BlockSpec(memory_space=pltpu.VMEM),
    )(flags, *sources)


def gain_as_rows(gain):
    high = lax.reduce_precision(gain, 8, 7)
    middle = lax.reduce_precision(gain - high, 8, 7)
    low = lax.reduce_precision(gain - high - middle, 8, 7)
    rows = jnp.stack([high, middle, low]).astype(BF)
    return jnp.pad(rows, ((0, GAIN_ROWS - 3), (0, 0)))


def on_device(node_feats, self_tiles, cross_tiles, cross_live, w_self, w_nbr, w_out, norm_gain):
    segment = lax.axis_index("segment")
    member = segment % MEMBERS
    here = segment * BLOCKS + lax.axis_index("node")
    flags = lax.dynamic_slice_in_dim(jnp.asarray(flag_table()), here, 1)[0]

    packed = jnp.concatenate([w_self[0], w_nbr[0], w_out[0], gain_as_rows(norm_gain[0])], axis=0)
    weights = [lax.ppermute(packed, AXES, weight_route(slot)) for slot in range(SLOTS)]

    live = cross_live[member].astype(BF)[:, :, None]
    sent = jnp.concatenate(
        [node_feats[member], self_tiles[member], cross_tiles[member] * live], axis=-1
    )
    sent = jnp.broadcast_to(sent[:, None], (4, 2) + sent.shape[1:]).reshape((8,) + sent.shape[1:])
    gathered = lax.all_to_all(sent, "node", 0, 0, tiled=True)

    outs = [None] * SLOTS
    state = None
    for t in range(len(STAGES)):
        slot = 0
        for group in STAGES[t][1]:
            slots = range(slot, slot + len(group))
            old = [outs[s] for s in slots if outs[s] is not None]
            new = run_layers(
                t, slot, flags, gathered, packed, state, [weights[s] for s in slots], old
            )
            for s, out in zip(slots, new):
                outs[s] = out
            slot += len(group)
            state = new[-1]
        if t < len(STAGES) - 1:
            state = lax.ppermute(state, AXES, stage_route(t))

    every = range(len(STAGES))
    sources = [lax.ppermute(outs[s], AXES, result_route(s, every)) for s in range(SLOTS)]
    home = pick(flags, sources + outs)
    spread = lax.all_to_all(home, "node", 0, 0, tiled=True)
    return spread.reshape(1, 4, 2, TILE, D)[:, :, 0]


def solution(mesh):
    return jax.shard_map(
        on_device,
        mesh=mesh,
        in_specs=(
            P(None, None, "node", None),
            P(None, None, "node", None),
            P(None, None, "node", None),
            P(None, None, "node"),
            P("segment", None, None),
            P("segment", None, None),
            P("segment", None, None),
            P("segment", None),
        ),
        out_specs=P("segment", None, "node", None),
        check_vma=False,
    )
```

```python
import functools

import jax
import jax.numpy as jnp
import numpy as np
from jax import lax
from jax.experimental import pallas as pl
from jax.experimental.pallas import tpu as pltpu
from jax.sharding import PartitionSpec as P

BF = jnp.bfloat16
F32 = jnp.float32
D = 512
TILE = 128
BLOCKS = 8
CHUNK = 4
MEMBERS = 4
AXES = ("segment", "node")
GAIN_ROWS = 16

STAGES = (
    (((0, 0), (0, 1), (0, 2), (0, 3)), ((0, 1), (2, 3, 4))),
    (((1, 0), (1, 1), (1, 2), (1, 3)), ((5, 6, 7, 8, 9, 10),)),
    (((3, 0), (2, 1), (3, 2), (2, 3)), ((11, 12, 13), (14, 15))),
)


def layers_of(t):
    return [layer for group in STAGES[t][1] for layer in group]


SLOTS = max(len(layers_of(t)) for t in range(len(STAGES)))
DEVICES = 512


def device(x, a, m, y, c):
    return (x * 16 + a * 4 + m) * BLOCKS + y * 2 + c


def over_chains(fn):
    pairs = [fn(m, y) for m in range(MEMBERS) for y in range(4)]
    return [(source, target) for source, target in pairs if source != target]


def chain(t, m, y):
    x, a = STAGES[t][0][m]
    return device(x, a, m, y, 0)


def home_of(layer, m, y):
    return device(layer // 4, layer % 4, m, y, 0)


def weight_route(slot):
    route = []
    for t in range(len(STAGES)):
        if slot < len(layers_of(t)):
            layer = layers_of(t)[slot]
            route += over_chains(lambda m, y: (home_of(layer, m, y), chain(t, m, y)))
    return route


def result_route(slot, stages):
    route = []
    for t in stages:
        if slot < len(layers_of(t)):
            layer = layers_of(t)[slot]
            route += over_chains(lambda m, y: (chain(t, m, y), home_of(layer, m, y)))
    return route


def stage_route(t):
    return over_chains(lambda m, y: (chain(t, m, y), chain(t + 1, m, y)))


STAGE_WIDTH = 1 + SLOTS
PICK_AT = len(STAGES) * STAGE_WIDTH


def flag_table():
    table = np.zeros((DEVICES, PICK_AT + 1), np.int32)
    for t in range(len(STAGES)):
        for m in range(MEMBERS):
            for y in range(4):
                at = chain(t, m, y)
                table[at, t * STAGE_WIDTH] = 1
                for slot, layer in enumerate(layers_of(t)):
                    home = home_of(layer, m, y)
                    table[at, t * STAGE_WIDTH + 1 + slot] = int(home == at)
                    table[home, PICK_AT] = slot + (SLOTS if home == at else 0)
    return table


def layers_kernel(t, first_slot, count, aliased, kind_in, *refs):
    flags, gathered, packed = refs[:3]
    at = 3
    states = refs[at : at + (0 if kind_in == "gathered" else 1)]
    at += len(states)
    weights = refs[at : at + count]
    at += count + aliased
    outs = refs[at : at + count]
    held, tiles, nodes, trunk, in_sems, out_sems = refs[at + count :]
    base = t * STAGE_WIDTH

    @pl.when(flags[base] == 1)
    def _():
        source = gathered.at[:, :, pl.ds(0, D)] if kind_in == "gathered" else states[0]
        state_copy = pltpu.make_async_copy(
            source, nodes.at[0, pl.ds(1, BLOCKS)], in_sems.at[count + 1]
        )
        tile_copy = pltpu.make_async_copy(
            gathered.at[:, :, pl.ds(D, 2 * TILE)], tiles, in_sems.at[count]
        )
        weight_copies = [
            pltpu.make_async_copy(weights[i], held.at[i], in_sems.at[i]) for i in range(count)
        ]

        def fetch(i):
            own = pltpu.make_async_copy(packed, held.at[i], in_sems.at[i])
            mine = flags[base + 1 + first_slot + i]
            pl.when(mine == 1)(own.start)
            pl.when(mine == 0)(weight_copies[i].start)

        state_copy.start()
        tile_copy.start()
        fetch(0)
        state_copy.wait()
        nodes[0, 0] = nodes[0, BLOCKS]
        tile_copy.wait()
        earlier = None
        for i in range(count):
            now = i % 2
            later = 1 - now
            weight_copies[i].wait()
            if i == 0:
                for j in range(1, count):
                    fetch(j)
            gain = held[i, 3 * D : 3 * D + GAIN_ROWS, :].astype(F32)
            gain = gain[0:1] + gain[1:2] + gain[2:3]
            for first in range(0, BLOCKS, CHUNK):
                sums = []
                for k in range(first, first + CHUNK):
                    both = jnp.concatenate(
                        [tiles[(k - 1) % BLOCKS, :, TILE:], tiles[k, :, :TILE]], axis=1
                    )
                    pair = nodes[now, k : k + 2].reshape(2 * TILE, D)
                    sums.append(jnp.dot(both, pair, preferred_element_type=F32).astype(BF))
                agg = jnp.concatenate(sums, axis=0)
                own = nodes[now, 1 + first : 1 + first + CHUNK].reshape(CHUNK * TILE, D)
                pre = jnp.dot(own, held[i, 0:D, :], preferred_element_type=F32)
                pre = pre + jnp.dot(agg, held[i, D : 2 * D, :], preferred_element_type=F32)
                hidden = jax.nn.silu(pre).astype(BF)
                if i == 0:
                    before = own.astype(F32)
                else:
                    before = trunk[first : first + CHUNK].reshape(CHUNK * TILE, D)
                value = before + jnp.dot(
                    hidden, held[i, 2 * D : 3 * D, :], preferred_element_type=F32
                )
                scale = lax.rsqrt(jnp.mean(value * value, axis=-1, keepdims=True) + 1e-06)
                updated = (value * scale * gain).reshape(CHUNK, TILE, D)
                if i < count - 1:
                    trunk[first : first + CHUNK] = updated
                new_nodes = updated.astype(BF)
                nodes[later, 1 + first : 1 + first + CHUNK] = new_nodes
                if first + CHUNK == BLOCKS and i < count - 1:
                    nodes[later, 0] = new_nodes[CHUNK - 1]
            copy = pltpu.make_async_copy(
                nodes.at[later, pl.ds(1, BLOCKS)], outs[i], out_sems.at[later]
            )
            copy.start()
            if earlier is not None:
                earlier.wait()
            earlier = copy
        earlier.wait()


def run_layers(t, first_slot, flags, gathered, packed, state, weights, outs):
    count = len(weights)
    kind_in = "gathered" if state is None else "bf16"
    states = [] if state is None else [state]
    where = pl.BlockSpec(memory_space=pltpu.HBM)
    n_in = 3 + len(states) + count
    return pl.pallas_call(
        functools.partial(layers_kernel, t, first_slot, count, len(outs), kind_in),
        out_shape=[jax.ShapeDtypeStruct((BLOCKS, TILE, D), BF)] * count,
        in_specs=[pl.BlockSpec(memory_space=pltpu.SMEM)] + [where] * (n_in - 1 + len(outs)),
        out_specs=[where] * count,
        input_output_aliases={n_in + i: i for i in range(len(outs))},
        scratch_shapes=[
            pltpu.VMEM((count, 3 * D + GAIN_ROWS, D), BF),
            pltpu.VMEM((BLOCKS, TILE, 2 * TILE), BF),
            pltpu.VMEM((2, BLOCKS + 1, TILE, D), BF),
            pltpu.VMEM((BLOCKS, TILE, D), F32),
            pltpu.SemaphoreType.DMA((count + 2,)),
            pltpu.SemaphoreType.DMA((2,)),
        ],
        compiler_params=pltpu.CompilerParams(vmem_limit_bytes=62 << 20),
        cost_estimate=pl.CostEstimate(
            flops=count * 1_880_000_000, bytes_accessed=count * 4_000_000, transcendentals=0
        ),
    )(flags, gathered, packed, *states, *weights, *outs)


def pick_kernel(flags, *refs):
    out = refs[-1]
    for i, source in enumerate(refs[:-1]):
        @pl.when(flags[PICK_AT] == i)
        def _():
            pltpu.sync_copy(source, out)


def pick(flags, sources):
    return pl.pallas_call(
        pick_kernel,
        out_shape=jax.ShapeDtypeStruct(sources[0].shape, sources[0].dtype),
        in_specs=[pl.BlockSpec(memory_space=pltpu.SMEM)]
        + [pl.BlockSpec(memory_space=pltpu.HBM)] * len(sources),
        out_specs=pl.BlockSpec(memory_space=pltpu.VMEM),
    )(flags, *sources)


def gain_as_rows(gain):
    high = lax.reduce_precision(gain, 8, 7)
    middle = lax.reduce_precision(gain - high, 8, 7)
    low = lax.reduce_precision(gain - high - middle, 8, 7)
    rows = jnp.stack([high, middle, low]).astype(BF)
    return jnp.pad(rows, ((0, GAIN_ROWS - 3), (0, 0)))


def on_device(node_feats, self_tiles, cross_tiles, cross_live, w_self, w_nbr, w_out, norm_gain):
    segment = lax.axis_index("segment")
    member = segment % MEMBERS
    here = segment * BLOCKS + lax.axis_index("node")
    flags = lax.dynamic_slice_in_dim(jnp.asarray(flag_table()), here, 1)[0]

    packed = jnp.concatenate([w_self[0], w_nbr[0], w_out[0], gain_as_rows(norm_gain[0])], axis=0)
    weights = [lax.ppermute(packed, AXES, weight_route(slot)) for slot in range(SLOTS)]

    live = cross_live[member].astype(BF)[:, :, None]
    sent = jnp.concatenate(
        [node_feats[member], self_tiles[member], cross_tiles[member] * live], axis=-1
    )
    sent = jnp.broadcast_to(sent[:, None], (4, 2) + sent.shape[1:]).reshape((8,) + sent.shape[1:])
    gathered = lax.all_to_all(sent, "node", 0, 0, tiled=True)

    outs = [None] * SLOTS
    state = None
    for t in range(len(STAGES)):
        slot = 0
        for group in STAGES[t][1]:
            slots = range(slot, slot + len(group))
            old = [outs[s] for s in slots if outs[s] is not None]
            new = run_layers(
                t, slot, flags, gathered, packed, state, [weights[s] for s in slots], old
            )
            for s, out in zip(slots, new):
                outs[s] = out
            slot += len(group)
            state = new[-1]
        if t < len(STAGES) - 1:
            state = lax.ppermute(state, AXES, stage_route(t))

    every = range(len(STAGES))
    sources = [lax.ppermute(outs[s], AXES, result_route(s, every)) for s in range(SLOTS)]
    home = pick(flags, sources + outs)
    spread = lax.all_to_all(home, "node", 0, 0, tiled=True)
    return spread.reshape(1, 4, 2, TILE, D)[:, :, 0]


def solution(mesh):
    return jax.shard_map(
        on_device,
        mesh=mesh,
        in_specs=(
            P(None, None, "node", None),
            P(None, None, "node", None),
            P(None, None, "node", None),
            P(None, None, "node"),
            P("segment", None, None),
            P("segment", None, None),
            P("segment", None, None),
            P("segment", None),
        ),
        out_specs=P("segment", None, "node", None),
        check_vma=False,
    )
```

```python
import functools

import jax
import jax.numpy as jnp
import numpy as np
from jax import lax
from jax.experimental import pallas as pl
from jax.experimental.pallas import tpu as pltpu
from jax.sharding import PartitionSpec as P

BF = jnp.bfloat16
F32 = jnp.float32
D = 512
TILE = 128
BLOCKS = 8
CHUNK = 4
MEMBERS = 4
AXES = ("segment", "node")
GAIN_ROWS = 16

STAGES = (
    (((0, 6), (0, 14), (0, 10), (0, 2)), ((0, 1), (2, 3, 4))),
    (((1, 6), (1, 14), (1, 10), (1, 2)), ((5, 6, 7, 8, 9, 10),)),
    (((3, 9), (3, 1), (2, 12), (1, 3)), ((11, 12, 13), (14, 15))),
)
RELEASES = ((0, 1), (2,))


def layers_of(t):
    return [layer for group in STAGES[t][1] for layer in group]


SLOTS = max(len(layers_of(t)) for t in range(len(STAGES)))
DEVICES = 512


def device(x, z, y, c):
    return (x * 16 + z) * BLOCKS + y * 2 + c


def over_chains(fn):
    pairs = [fn(m, y) for m in range(MEMBERS) for y in range(4)]
    return [(source, target) for source, target in pairs if source != target]


def chain(t, m, y):
    x, z = STAGES[t][0][m]
    return device(x, z, y, 0)


def home_of(layer, m, y):
    return device(layer // 4, layer % 4 * 4 + m, y, 0)


def weight_route(slot):
    route = []
    for t in range(len(STAGES)):
        if slot < len(layers_of(t)):
            layer = layers_of(t)[slot]
            route += over_chains(lambda m, y: (home_of(layer, m, y), chain(t, m, y)))
    return route


def slots_of(release):
    return max(len(layers_of(t)) for t in release)


def result_route(slot, release):
    route = []
    for t in release:
        if slot < len(layers_of(t)):
            layer = layers_of(t)[slot]
            route += over_chains(lambda m, y: (chain(t, m, y), home_of(layer, m, y)))
    return route


def stage_route(t):
    return over_chains(lambda m, y: (chain(t, m, y), chain(t + 1, m, y)))


STAGE_WIDTH = 1 + SLOTS
PICK_AT = len(STAGES) * STAGE_WIDTH
MEMBER_AT = PICK_AT + 1


def flag_table():
    table = np.zeros((DEVICES, MEMBER_AT + 1), np.int32)
    offset = 0
    arriving = sum(slots_of(release) for release in RELEASES)
    for release in RELEASES:
        for t in release:
            for m in range(MEMBERS):
                for y in range(4):
                    at = chain(t, m, y)
                    table[at : at + 2, MEMBER_AT] = m
                    table[at, t * STAGE_WIDTH] = 1
                    for slot, layer in enumerate(layers_of(t)):
                        home = home_of(layer, m, y)
                        table[at, t * STAGE_WIDTH + 1 + slot] = int(home == at)
                        table[home, PICK_AT] = offset + slot + (arriving if home == at else 0)
        offset += slots_of(release)
    return table


def layers_kernel(t, first_slot, count, aliased, kind_in, *refs):
    flags, gathered, packed = refs[:3]
    at = 3
    states = refs[at : at + (0 if kind_in == "gathered" else 1)]
    at += len(states)
    weights = refs[at : at + count]
    at += count + aliased
    outs = refs[at : at + count]
    held, tiles, nodes, trunk, in_sems, out_sems = refs[at + count :]
    base = t * STAGE_WIDTH

    @pl.when(flags[base] == 1)
    def _():
        source = gathered.at[:, :, pl.ds(0, D)] if kind_in == "gathered" else states[0]
        state_copy = pltpu.make_async_copy(
            source, nodes.at[0, pl.ds(1, BLOCKS)], in_sems.at[count + 1]
        )
        tile_copy = pltpu.make_async_copy(
            gathered.at[:, :, pl.ds(D, 2 * TILE)], tiles, in_sems.at[count]
        )
        weight_copies = [
            pltpu.make_async_copy(weights[i], held.at[i], in_sems.at[i]) for i in range(count)
        ]

        def fetch(i):
            own = pltpu.make_async_copy(packed, held.at[i], in_sems.at[i])
            mine = flags[base + 1 + first_slot + i]
            pl.when(mine == 1)(own.start)
            pl.when(mine == 0)(weight_copies[i].start)

        state_copy.start()
        tile_copy.start()
        fetch(0)
        state_copy.wait()
        nodes[0, 0] = nodes[0, BLOCKS]
        tile_copy.wait()
        earlier = None
        for i in range(count):
            now = i % 2
            later = 1 - now
            weight_copies[i].wait()
            if i == 0:
                for j in range(1, count):
                    fetch(j)
            gain = held[i, 3 * D : 3 * D + GAIN_ROWS, :].astype(F32)
            gain = gain[0:1] + gain[1:2] + gain[2:3]
            for first in range(0, BLOCKS, CHUNK):
                sums = []
                for k in range(first, first + CHUNK):
                    both = jnp.concatenate(
                        [tiles[(k - 1) % BLOCKS, :, TILE:], tiles[k, :, :TILE]], axis=1
                    )
                    pair = nodes[now, k : k + 2].reshape(2 * TILE, D)
                    sums.append(jnp.dot(both, pair, preferred_element_type=F32).astype(BF))
                agg = jnp.concatenate(sums, axis=0)
                own = nodes[now, 1 + first : 1 + first + CHUNK].reshape(CHUNK * TILE, D)
                pre = jnp.dot(own, held[i, 0:D, :], preferred_element_type=F32)
                pre = pre + jnp.dot(agg, held[i, D : 2 * D, :], preferred_element_type=F32)
                hidden = jax.nn.silu(pre).astype(BF)
                if i == 0:
                    before = own.astype(F32)
                else:
                    before = trunk[first : first + CHUNK].reshape(CHUNK * TILE, D)
                value = before + jnp.dot(
                    hidden, held[i, 2 * D : 3 * D, :], preferred_element_type=F32
                )
                scale = lax.rsqrt(jnp.mean(value * value, axis=-1, keepdims=True) + 1e-06)
                updated = (value * scale * gain).reshape(CHUNK, TILE, D)
                if i < count - 1:
                    trunk[first : first + CHUNK] = updated
                new_nodes = updated.astype(BF)
                nodes[later, 1 + first : 1 + first + CHUNK] = new_nodes
                if first + CHUNK == BLOCKS and i < count - 1:
                    nodes[later, 0] = new_nodes[CHUNK - 1]
            copy = pltpu.make_async_copy(
                nodes.at[later, pl.ds(1, BLOCKS)], outs[i], out_sems.at[later]
            )
            copy.start()
            if earlier is not None:
                earlier.wait()
            earlier = copy
        earlier.wait()


def run_layers(t, first_slot, flags, gathered, packed, state, weights, outs):
    count = len(weights)
    kind_in = "gathered" if state is None else "bf16"
    states = [] if state is None else [state]
    where = pl.BlockSpec(memory_space=pltpu.HBM)
    n_in = 3 + len(states) + count
    return pl.pallas_call(
        functools.partial(layers_kernel, t, first_slot, count, len(outs), kind_in),
        out_shape=[jax.ShapeDtypeStruct((BLOCKS, TILE, D), BF)] * count,
        in_specs=[pl.BlockSpec(memory_space=pltpu.SMEM)] + [where] * (n_in - 1 + len(outs)),
        out_specs=[where] * count,
        input_output_aliases={n_in + i: i for i in range(len(outs))},
        scratch_shapes=[
            pltpu.VMEM((count, 3 * D + GAIN_ROWS, D), BF),
            pltpu.VMEM((BLOCKS, TILE, 2 * TILE), BF),
            pltpu.VMEM((2, BLOCKS + 1, TILE, D), BF),
            pltpu.VMEM((BLOCKS, TILE, D), F32),
            pltpu.SemaphoreType.DMA((count + 2,)),
            pltpu.SemaphoreType.DMA((2,)),
        ],
        compiler_params=pltpu.CompilerParams(vmem_limit_bytes=62 << 20),
        cost_estimate=pl.CostEstimate(
            flops=count * 1_880_000_000, bytes_accessed=count * 4_000_000, transcendentals=0
        ),
    )(flags, gathered, packed, *states, *weights, *outs)


def pick_kernel(flags, *refs):
    out = refs[-1]
    for i, source in enumerate(refs[:-1]):
        @pl.when(flags[PICK_AT] == i)
        def _():
            pltpu.sync_copy(source, out)


def pick(flags, sources):
    return pl.pallas_call(
        pick_kernel,
        out_shape=jax.ShapeDtypeStruct(sources[0].shape, sources[0].dtype),
        in_specs=[pl.BlockSpec(memory_space=pltpu.SMEM)]
        + [pl.BlockSpec(memory_space=pltpu.HBM)] * len(sources),
        out_specs=pl.BlockSpec(memory_space=pltpu.VMEM),
    )(flags, *sources)


def gain_as_rows(gain):
    high = lax.reduce_precision(gain, 8, 7)
    middle = lax.reduce_precision(gain - high, 8, 7)
    low = lax.reduce_precision(gain - high - middle, 8, 7)
    rows = jnp.stack([high, middle, low]).astype(BF)
    return jnp.pad(rows, ((0, GAIN_ROWS - 3), (0, 0)))


def on_device(node_feats, self_tiles, cross_tiles, cross_live, w_self, w_nbr, w_out, norm_gain):
    here = lax.axis_index("segment") * BLOCKS + lax.axis_index("node")
    flags = lax.dynamic_slice_in_dim(jnp.asarray(flag_table()), here, 1)[0]
    member = flags[MEMBER_AT]

    packed = jnp.concatenate([w_self[0], w_nbr[0], w_out[0], gain_as_rows(norm_gain[0])], axis=0)
    weights = [lax.ppermute(packed, AXES, weight_route(slot)) for slot in range(SLOTS)]

    live = cross_live[member].astype(BF)[:, :, None]
    sent = jnp.concatenate(
        [node_feats[member], self_tiles[member], cross_tiles[member] * live], axis=-1
    )
    sent = jnp.broadcast_to(sent[:, None], (4, 2) + sent.shape[1:]).reshape((8,) + sent.shape[1:])
    gathered = lax.all_to_all(sent, "node", 0, 0, tiled=True)

    arrived = []
    kept = []
    state = None
    for release in RELEASES:
        outs = [None] * slots_of(release)
        for t in release:
            slot = 0
            for group in STAGES[t][1]:
                slots = range(slot, slot + len(group))
                old = [outs[s] for s in slots if outs[s] is not None]
                new = run_layers(
                    t, slot, flags, gathered, packed, state, [weights[s] for s in slots], old
                )
                for s, out in zip(slots, new):
                    outs[s] = out
                slot += len(group)
                state = new[-1]
            if t < len(STAGES) - 1:
                state = lax.ppermute(state, AXES, stage_route(t))
        kept += outs
        arrived += [lax.ppermute(out, AXES, result_route(s, release)) for s, out in enumerate(outs)]

    home = pick(flags, arrived + kept)
    spread = lax.all_to_all(home, "node", 0, 0, tiled=True)
    return spread.reshape(1, 4, 2, TILE, D)[:, :, 0]


def solution(mesh):
    return jax.shard_map(
        on_device,
        mesh=mesh,
        in_specs=(
            P(None, None, "node", None),
            P(None, None, "node", None),
            P(None, None, "node", None),
            P(None, None, "node"),
            P("segment", None, None),
            P("segment", None, None),
            P("segment", None, None),
            P("segment", None),
        ),
        out_specs=P("segment", None, "node", None),
        check_vma=False,
    )
```

```python
import functools

import jax
import jax.numpy as jnp
import numpy as np
from jax import lax
from jax.experimental import pallas as pl
from jax.experimental.pallas import tpu as pltpu
from jax.sharding import PartitionSpec as P

BF = jnp.bfloat16
F32 = jnp.float32
D = 512
TILE = 128
BLOCKS = 8
CHUNK = 4
MEMBERS = 4
AXES = ("segment", "node")
GAIN_ROWS = 16

STAGES = (
    (((0, 6), (0, 14), (0, 10), (0, 2)), ((0, 1), (2, 3, 4))),
    (((1, 6), (1, 14), (1, 10), (1, 2)), ((5, 6, 7, 8, 9, 10),)),
    (((3, 9), (3, 1), (2, 12), (1, 3)), ((11, 12, 13), (14, 15))),
)
RELEASES = ((0, 1, 2),)


def layers_of(t):
    return [layer for group in STAGES[t][1] for layer in group]


SLOTS = max(len(layers_of(t)) for t in range(len(STAGES)))
DEVICES = 512


def device(x, z, y, c):
    return (x * 16 + z) * BLOCKS + y * 2 + c


def over_chains(fn):
    pairs = [fn(m, y) for m in range(MEMBERS) for y in range(4)]
    return [(source, target) for source, target in pairs if source != target]


def chain(t, m, y):
    x, z = STAGES[t][0][m]
    return device(x, z, y, 1)


def home_of(layer, m, y):
    return device(layer // 4, layer % 4 * 4 + m, y, 0)


def weight_route(slot):
    route = []
    for t in range(len(STAGES)):
        if slot < len(layers_of(t)):
            layer = layers_of(t)[slot]
            route += over_chains(lambda m, y: (home_of(layer, m, y), chain(t, m, y)))
    return route


def slots_of(release):
    return max(len(layers_of(t)) for t in release)


def result_route(slot, release):
    route = []
    for t in release:
        if slot < len(layers_of(t)):
            layer = layers_of(t)[slot]
            route += over_chains(lambda m, y: (chain(t, m, y), home_of(layer, m, y)))
    return route


def stage_route(t):
    return over_chains(lambda m, y: (chain(t, m, y), chain(t + 1, m, y)))


PICK_AT = len(STAGES)
MEMBER_AT = PICK_AT + 1


def flag_table():
    table = np.zeros((DEVICES, MEMBER_AT + 1), np.int32)
    offset = 0
    for release in RELEASES:
        for t in release:
            for m in range(MEMBERS):
                for y in range(4):
                    at = chain(t, m, y)
                    table[at - 1 : at + 1, MEMBER_AT] = m
                    table[at, t] = 1
                    for slot, layer in enumerate(layers_of(t)):
                        table[home_of(layer, m, y), PICK_AT] = offset + slot
        offset += slots_of(release)
    return table


def layers_kernel(t, count, aliased, kind_in, *refs):
    flags, gathered = refs[:2]
    at = 2
    states = refs[at : at + (0 if kind_in == "gathered" else 1)]
    at += len(states)
    weights = refs[at : at + count]
    at += count + aliased
    outs = refs[at : at + count]
    held, tiles, nodes, trunk, in_sems, out_sems = refs[at + count :]

    @pl.when(flags[t] == 1)
    def _():
        source = gathered.at[:, :, pl.ds(0, D)] if kind_in == "gathered" else states[0]
        state_copy = pltpu.make_async_copy(
            source, nodes.at[0, pl.ds(1, BLOCKS)], in_sems.at[count + 1]
        )
        tile_copy = pltpu.make_async_copy(
            gathered.at[:, :, pl.ds(D, 2 * TILE)], tiles, in_sems.at[count]
        )
        weight_copies = [
            pltpu.make_async_copy(weights[i], held.at[i], in_sems.at[i]) for i in range(count)
        ]
        state_copy.start()
        tile_copy.start()
        weight_copies[0].start()
        state_copy.wait()
        nodes[0, 0] = nodes[0, BLOCKS]
        tile_copy.wait()
        earlier = None
        for i in range(count):
            now = i % 2
            later = 1 - now
            weight_copies[i].wait()
            if i == 0:
                for j in range(1, count):
                    weight_copies[j].start()
            gain = held[i, 3 * D : 3 * D + GAIN_ROWS, :].astype(F32)
            gain = gain[0:1] + gain[1:2] + gain[2:3]
            for first in range(0, BLOCKS, CHUNK):
                sums = []
                for k in range(first, first + CHUNK):
                    both = jnp.concatenate(
                        [tiles[(k - 1) % BLOCKS, :, TILE:], tiles[k, :, :TILE]], axis=1
                    )
                    pair = nodes[now, k : k + 2].reshape(2 * TILE, D)
                    sums.append(jnp.dot(both, pair, preferred_element_type=F32).astype(BF))
                agg = jnp.concatenate(sums, axis=0)
                own = nodes[now, 1 + first : 1 + first + CHUNK].reshape(CHUNK * TILE, D)
                pre = jnp.dot(own, held[i, 0:D, :], preferred_element_type=F32)
                pre = pre + jnp.dot(agg, held[i, D : 2 * D, :], preferred_element_type=F32)
                hidden = jax.nn.silu(pre).astype(BF)
                if i == 0:
                    before = own.astype(F32)
                else:
                    before = trunk[first : first + CHUNK].reshape(CHUNK * TILE, D)
                value = before + jnp.dot(
                    hidden, held[i, 2 * D : 3 * D, :], preferred_element_type=F32
                )
                scale = lax.rsqrt(jnp.mean(value * value, axis=-1, keepdims=True) + 1e-06)
                updated = (value * scale * gain).reshape(CHUNK, TILE, D)
                if i < count - 1:
                    trunk[first : first + CHUNK] = updated
                new_nodes = updated.astype(BF)
                nodes[later, 1 + first : 1 + first + CHUNK] = new_nodes
                if first + CHUNK == BLOCKS and i < count - 1:
                    nodes[later, 0] = new_nodes[CHUNK - 1]
            copy = pltpu.make_async_copy(
                nodes.at[later, pl.ds(1, BLOCKS)], outs[i], out_sems.at[later]
            )
            copy.start()
            if earlier is not None:
                earlier.wait()
            earlier = copy
        earlier.wait()


def run_layers(t, flags, gathered, state, weights, outs):
    count = len(weights)
    kind_in = "gathered" if state is None else "bf16"
    states = [] if state is None else [state]
    where = pl.BlockSpec(memory_space=pltpu.HBM)
    n_in = 2 + len(states) + count
    return pl.pallas_call(
        functools.partial(layers_kernel, t, count, len(outs), kind_in),
        out_shape=[jax.ShapeDtypeStruct((BLOCKS, TILE, D), BF)] * count,
        in_specs=[pl.BlockSpec(memory_space=pltpu.SMEM)] + [where] * (n_in - 1 + len(outs)),
        out_specs=[where] * count,
        input_output_aliases={n_in + i: i for i in range(len(outs))},
        scratch_shapes=[
            pltpu.VMEM((count, 3 * D + GAIN_ROWS, D), BF),
            pltpu.VMEM((BLOCKS, TILE, 2 * TILE), BF),
            pltpu.VMEM((2, BLOCKS + 1, TILE, D), BF),
            pltpu.VMEM((BLOCKS, TILE, D), F32),
            pltpu.SemaphoreType.DMA((count + 2,)),
            pltpu.SemaphoreType.DMA((2,)),
        ],
        compiler_params=pltpu.CompilerParams(vmem_limit_bytes=62 << 20),
        cost_estimate=pl.CostEstimate(
            flops=count * 1_880_000_000, bytes_accessed=count * 4_000_000, transcendentals=0
        ),
    )(flags, gathered, *states, *weights, *outs)


def pick_kernel(flags, *refs):
    out = refs[-1]
    for i, source in enumerate(refs[:-1]):
        @pl.when(flags[PICK_AT] == i)
        def _():
            pltpu.sync_copy(source, out)


def pick(flags, sources):
    return pl.pallas_call(
        pick_kernel,
        out_shape=jax.ShapeDtypeStruct(sources[0].shape, sources[0].dtype),
        in_specs=[pl.BlockSpec(memory_space=pltpu.SMEM)]
        + [pl.BlockSpec(memory_space=pltpu.HBM)] * len(sources),
        out_specs=pl.BlockSpec(memory_space=pltpu.VMEM),
    )(flags, *sources)


def gain_as_rows(gain):
    high = lax.reduce_precision(gain, 8, 7)
    middle = lax.reduce_precision(gain - high, 8, 7)
    low = lax.reduce_precision(gain - high - middle, 8, 7)
    rows = jnp.stack([high, middle, low]).astype(BF)
    return jnp.pad(rows, ((0, GAIN_ROWS - 3), (0, 0)))


def on_device(node_feats, self_tiles, cross_tiles, cross_live, w_self, w_nbr, w_out, norm_gain):
    here = lax.axis_index("segment") * BLOCKS + lax.axis_index("node")
    flags = lax.dynamic_slice_in_dim(jnp.asarray(flag_table()), here, 1)[0]
    member = flags[MEMBER_AT]

    packed = jnp.concatenate([w_self[0], w_nbr[0], w_out[0], gain_as_rows(norm_gain[0])], axis=0)
    weights = [lax.ppermute(packed, AXES, weight_route(slot)) for slot in range(SLOTS)]

    live = cross_live[member].astype(BF)[:, :, None]
    sent = jnp.concatenate(
        [node_feats[member], self_tiles[member], cross_tiles[member] * live], axis=-1
    )
    sent = jnp.broadcast_to(sent[:, None], (4, 2) + sent.shape[1:]).reshape((8,) + sent.shape[1:])
    gathered = lax.all_to_all(sent, "node", 0, 0, tiled=True)

    arrived = []
    state = None
    for release in RELEASES:
        outs = [None] * slots_of(release)
        for t in release:
            slot = 0
            for group in STAGES[t][1]:
                slots = range(slot, slot + len(group))
                old = [outs[s] for s in slots if outs[s] is not None]
                new = run_layers(
                    t, flags, gathered, state, [weights[s] for s in slots], old
                )
                for s, out in zip(slots, new):
                    outs[s] = out
                slot += len(group)
                state = new[-1]
            if t < len(STAGES) - 1:
                state = lax.ppermute(state, AXES, stage_route(t))
        arrived += [lax.ppermute(out, AXES, result_route(s, release)) for s, out in enumerate(outs)]

    home = pick(flags, arrived)
    spread = lax.all_to_all(home, "node", 0, 0, tiled=True)
    return spread.reshape(1, 4, 2, TILE, D)[:, :, 0]


def solution(mesh):
    return jax.shard_map(
        on_device,
        mesh=mesh,
        in_specs=(
            P(None, None, "node", None),
            P(None, None, "node", None),
            P(None, None, "node", None),
            P(None, None, "node"),
            P("segment", None, None),
            P("segment", None, None),
            P("segment", None, None),
            P("segment", None),
        ),
        out_specs=P("segment", None, "node", None),
        check_vma=False,
    )
```

```python
import functools

import jax
import jax.numpy as jnp
import numpy as np
from jax import lax
from jax.experimental import pallas as pl
from jax.experimental.pallas import tpu as pltpu
from jax.sharding import PartitionSpec as P

BF = jnp.bfloat16
F32 = jnp.float32
D = 512
TILE = 128
BLOCKS = 8
CHUNK = 4
MEMBERS = 4
AXES = ("segment", "node")
GAIN_ROWS = 16

STAGES = (
    (((0, 6), (0, 14), (0, 10), (0, 2)), ((0, 1), (2, 3, 4))),
    (((2, 6), (2, 14), (2, 10), (2, 2)), ((5, 6, 7, 8, 9, 10),)),
    (((3, 6), (3, 14), (1, 10), (1, 2)), ((11, 12, 13), (14, 15))),
)
SUPPLIES = ((0, 1, 2),)
RELEASES = ((0, 1, 2),)


def layers_of(t):
    return [layer for group in STAGES[t][1] for layer in group]


SLOTS = max(len(layers_of(t)) for t in range(len(STAGES)))
DEVICES = 512


def device(x, z, y, c):
    return (x * 16 + z) * BLOCKS + y * 2 + c


def over_chains(fn):
    pairs = [fn(m, y) for m in range(MEMBERS) for y in range(4)]
    return [(source, target) for source, target in pairs if source != target]


def chain(t, m, y):
    x, z = STAGES[t][0][m]
    return device(x, z, y, 1)


def home_of(layer, m, y):
    return device(layer // 4, layer % 4 * 4 + m, y, 0)


def weight_route(slot, supply):
    route = []
    for t in supply:
        if slot < len(layers_of(t)):
            layer = layers_of(t)[slot]
            route += over_chains(lambda m, y: (home_of(layer, m, y), chain(t, m, y)))
    return route


def slots_of(stages):
    return max(len(layers_of(t)) for t in stages)


def result_route(slot, release):
    route = []
    for t in release:
        if slot < len(layers_of(t)):
            layer = layers_of(t)[slot]
            route += over_chains(lambda m, y: (chain(t, m, y), home_of(layer, m, y)))
    return route


def stage_route(t):
    return over_chains(lambda m, y: (chain(t, m, y), chain(t + 1, m, y)))


PICK_AT = len(STAGES)
MEMBER_AT = PICK_AT + 1


def flag_table():
    table = np.zeros((DEVICES, MEMBER_AT + 1), np.int32)
    offset = 0
    for release in RELEASES:
        for t in release:
            for m in range(MEMBERS):
                for y in range(4):
                    at = chain(t, m, y)
                    table[at - 1 : at + 1, MEMBER_AT] = m
                    table[at, t] = 1
                    for slot, layer in enumerate(layers_of(t)):
                        table[home_of(layer, m, y), PICK_AT] = offset + slot
        offset += slots_of(release)
    return table


def layers_kernel(t, count, aliased, kind_in, *refs):
    flags, gathered = refs[:2]
    at = 2
    states = refs[at : at + (0 if kind_in == "gathered" else 1)]
    at += len(states)
    weights = refs[at : at + count]
    at += count + aliased
    outs = refs[at : at + count]
    held, tiles, nodes, trunk, in_sems, out_sems = refs[at + count :]

    @pl.when(flags[t] == 1)
    def _():
        source = gathered.at[:, :, pl.ds(0, D)] if kind_in == "gathered" else states[0]
        state_copy = pltpu.make_async_copy(
            source, nodes.at[0, pl.ds(1, BLOCKS)], in_sems.at[count + 1]
        )
        tile_copy = pltpu.make_async_copy(
            gathered.at[:, :, pl.ds(D, 2 * TILE)], tiles, in_sems.at[count]
        )
        weight_copies = [
            pltpu.make_async_copy(weights[i], held.at[i], in_sems.at[i]) for i in range(count)
        ]
        state_copy.start()
        tile_copy.start()
        weight_copies[0].start()
        state_copy.wait()
        nodes[0, 0] = nodes[0, BLOCKS]
        tile_copy.wait()
        earlier = None
        for i in range(count):
            now = i % 2
            later = 1 - now
            weight_copies[i].wait()
            if i == 0:
                for j in range(1, count):
                    weight_copies[j].start()
            gain = held[i, 3 * D : 3 * D + GAIN_ROWS, :].astype(F32)
            gain = gain[0:1] + gain[1:2] + gain[2:3]
            for first in range(0, BLOCKS, CHUNK):
                sums = []
                for k in range(first, first + CHUNK):
                    both = jnp.concatenate(
                        [tiles[(k - 1) % BLOCKS, :, TILE:], tiles[k, :, :TILE]], axis=1
                    )
                    pair = nodes[now, k : k + 2].reshape(2 * TILE, D)
                    sums.append(jnp.dot(both, pair, preferred_element_type=F32).astype(BF))
                agg = jnp.concatenate(sums, axis=0)
                own = nodes[now, 1 + first : 1 + first + CHUNK].reshape(CHUNK * TILE, D)
                pre = jnp.dot(own, held[i, 0:D, :], preferred_element_type=F32)
                pre = pre + jnp.dot(agg, held[i, D : 2 * D, :], preferred_element_type=F32)
                hidden = jax.nn.silu(pre).astype(BF)
                if i == 0:
                    before = own.astype(F32)
                else:
                    before = trunk[first : first + CHUNK].reshape(CHUNK * TILE, D)
                value = before + jnp.dot(
                    hidden, held[i, 2 * D : 3 * D, :], preferred_element_type=F32
                )
                scale = lax.rsqrt(jnp.mean(value * value, axis=-1, keepdims=True) + 1e-06)
                updated = (value * scale * gain).reshape(CHUNK, TILE, D)
                if i < count - 1:
                    trunk[first : first + CHUNK] = updated
                new_nodes = updated.astype(BF)
                nodes[later, 1 + first : 1 + first + CHUNK] = new_nodes
                if first + CHUNK == BLOCKS and i < count - 1:
                    nodes[later, 0] = new_nodes[CHUNK - 1]
            copy = pltpu.make_async_copy(
                nodes.at[later, pl.ds(1, BLOCKS)], outs[i], out_sems.at[later]
            )
            copy.start()
            if earlier is not None:
                earlier.wait()
            earlier = copy
        earlier.wait()


def run_layers(t, flags, gathered, state, weights, outs):
    count = len(weights)
    kind_in = "gathered" if state is None else "bf16"
    states = [] if state is None else [state]
    where = pl.BlockSpec(memory_space=pltpu.HBM)
    n_in = 2 + len(states) + count
    return pl.pallas_call(
        functools.partial(layers_kernel, t, count, len(outs), kind_in),
        out_shape=[jax.ShapeDtypeStruct((BLOCKS, TILE, D), BF)] * count,
        in_specs=[pl.BlockSpec(memory_space=pltpu.SMEM)] + [where] * (n_in - 1 + len(outs)),
        out_specs=[where] * count,
        input_output_aliases={n_in + i: i for i in range(len(outs))},
        scratch_shapes=[
            pltpu.VMEM((count, 3 * D + GAIN_ROWS, D), BF),
            pltpu.VMEM((BLOCKS, TILE, 2 * TILE), BF),
            pltpu.VMEM((2, BLOCKS + 1, TILE, D), BF),
            pltpu.VMEM((BLOCKS, TILE, D), F32),
            pltpu.SemaphoreType.DMA((count + 2,)),
            pltpu.SemaphoreType.DMA((2,)),
        ],
        compiler_params=pltpu.CompilerParams(vmem_limit_bytes=62 << 20),
        cost_estimate=pl.CostEstimate(
            flops=count * 1_880_000_000, bytes_accessed=count * 4_000_000, transcendentals=0
        ),
    )(flags, gathered, *states, *weights, *outs)


def pick_kernel(flags, *refs):
    out = refs[-1]
    for i, source in enumerate(refs[:-1]):
        @pl.when(flags[PICK_AT] == i)
        def _():
            pltpu.sync_copy(source, out)


def pick(flags, sources):
    return pl.pallas_call(
        pick_kernel,
        out_shape=jax.ShapeDtypeStruct(sources[0].shape, sources[0].dtype),
        in_specs=[pl.BlockSpec(memory_space=pltpu.SMEM)]
        + [pl.BlockSpec(memory_space=pltpu.HBM)] * len(sources),
        out_specs=pl.BlockSpec(memory_space=pltpu.VMEM),
    )(flags, *sources)


def gain_as_rows(gain):
    high = lax.reduce_precision(gain, 8, 7)
    middle = lax.reduce_precision(gain - high, 8, 7)
    low = lax.reduce_precision(gain - high - middle, 8, 7)
    rows = jnp.stack([high, middle, low]).astype(BF)
    return jnp.pad(rows, ((0, GAIN_ROWS - 3), (0, 0)))


def on_device(node_feats, self_tiles, cross_tiles, cross_live, w_self, w_nbr, w_out, norm_gain):
    here = lax.axis_index("segment") * BLOCKS + lax.axis_index("node")
    flags = lax.dynamic_slice_in_dim(jnp.asarray(flag_table()), here, 1)[0]
    member = flags[MEMBER_AT]

    packed = jnp.concatenate([w_self[0], w_nbr[0], w_out[0], gain_as_rows(norm_gain[0])], axis=0)
    weights = [None] * len(STAGES)
    for supply in SUPPLIES:
        sent = [lax.ppermute(packed, AXES, weight_route(s, supply)) for s in range(slots_of(supply))]
        for t in supply:
            weights[t] = sent

    live = cross_live[member].astype(BF)[:, :, None]
    sent = jnp.concatenate(
        [node_feats[member], self_tiles[member], cross_tiles[member] * live], axis=-1
    )
    sent = jnp.broadcast_to(sent[:, None], (4, 2) + sent.shape[1:]).reshape((8,) + sent.shape[1:])
    gathered = lax.all_to_all(sent, "node", 0, 0, tiled=True)

    arrived = []
    state = None
    for release in RELEASES:
        outs = [None] * slots_of(release)
        for t in release:
            slot = 0
            for group in STAGES[t][1]:
                slots = range(slot, slot + len(group))
                old = [outs[s] for s in slots if outs[s] is not None]
                new = run_layers(
                    t, flags, gathered, state, [weights[t][s] for s in slots], old
                )
                for s, out in zip(slots, new):
                    outs[s] = out
                slot += len(group)
                state = new[-1]
            if t < len(STAGES) - 1:
                state = lax.ppermute(state, AXES, stage_route(t))
        arrived += [lax.ppermute(out, AXES, result_route(s, release)) for s, out in enumerate(outs)]

    home = pick(flags, arrived)
    spread = lax.all_to_all(home, "node", 0, 0, tiled=True)
    return spread.reshape(1, 4, 2, TILE, D)[:, :, 0]


def solution(mesh):
    return jax.shard_map(
        on_device,
        mesh=mesh,
        in_specs=(
            P(None, None, "node", None),
            P(None, None, "node", None),
            P(None, None, "node", None),
            P(None, None, "node"),
            P("segment", None, None),
            P("segment", None, None),
            P("segment", None, None),
            P("segment", None),
        ),
        out_specs=P("segment", None, "node", None),
        check_vma=False,
    )
```

```python
import functools

import jax
import jax.numpy as jnp
import numpy as np
from jax import lax
from jax.experimental import pallas as pl
from jax.experimental.pallas import tpu as pltpu
from jax.sharding import PartitionSpec as P

BF = jnp.bfloat16
F32 = jnp.float32
D = 512
TILE = 128
BLOCKS = 8
CHUNK = 4
MEMBERS = 4
AXES = ("segment", "node")
GAIN_ROWS = 16

STAGES = (
    (((0, 11), (0, 2), (0, 5), (0, 13)), ((0, 1), (2, 3))),
    (((2, 11), (2, 2), (2, 5), (2, 13)), ((4, 5, 6, 7, 8, 9),)),
    (((3, 11), (3, 2), (1, 5), (1, 13)), ((10, 11, 12, 13), (14, 15))),
)
SUPPLIES = ((0, 1, 2),)
RELEASES = ((0, 1, 2),)


def layers_of(t):
    return [layer for group in STAGES[t][1] for layer in group]


SLOTS = max(len(layers_of(t)) for t in range(len(STAGES)))
DEVICES = 512


def device(x, z, y, c):
    return (x * 16 + z) * BLOCKS + y * 2 + c


def over_chains(fn):
    pairs = [fn(m, y) for m in range(MEMBERS) for y in range(4)]
    return [(source, target) for source, target in pairs if source != target]


def chain(t, m, y):
    x, z = STAGES[t][0][m]
    return device(x, z, y, 1)


def home_of(layer, m, y):
    return device(layer // 4, layer % 4 * 4 + m, y, 0)


def weight_route(slot, supply):
    route = []
    for t in supply:
        if slot < len(layers_of(t)):
            layer = layers_of(t)[slot]
            route += over_chains(lambda m, y: (home_of(layer, m, y), chain(t, m, y)))
    return route


def slots_of(stages):
    return max(len(layers_of(t)) for t in stages)


def result_route(slot, release):
    route = []
    for t in release:
        if slot < len(layers_of(t)):
            layer = layers_of(t)[slot]
            route += over_chains(lambda m, y: (chain(t, m, y), home_of(layer, m, y)))
    return route


def stage_route(t):
    return over_chains(lambda m, y: (chain(t, m, y), chain(t + 1, m, y)))


PICK_AT = len(STAGES)
MEMBER_AT = PICK_AT + 1


def flag_table():
    table = np.zeros((DEVICES, MEMBER_AT + 1), np.int32)
    offset = 0
    for release in RELEASES:
        for t in release:
            for m in range(MEMBERS):
                for y in range(4):
                    at = chain(t, m, y)
                    table[at - 1 : at + 1, MEMBER_AT] = m
                    table[at, t] = 1
                    for slot, layer in enumerate(layers_of(t)):
                        table[home_of(layer, m, y), PICK_AT] = offset + slot
        offset += slots_of(release)
    return table


def layers_kernel(t, count, aliased, kind_in, *refs):
    flags, gathered = refs[:2]
    at = 2
    states = refs[at : at + (0 if kind_in == "gathered" else 1)]
    at += len(states)
    weights = refs[at : at + count]
    at += count + aliased
    outs = refs[at : at + count]
    held, tiles, nodes, trunk, in_sems, out_sems = refs[at + count :]

    @pl.when(flags[t] == 1)
    def _():
        source = gathered.at[:, :, pl.ds(0, D)] if kind_in == "gathered" else states[0]
        state_copy = pltpu.make_async_copy(
            source, nodes.at[0, pl.ds(1, BLOCKS)], in_sems.at[count + 1]
        )
        tile_copy = pltpu.make_async_copy(
            gathered.at[:, :, pl.ds(D, 2 * TILE)], tiles, in_sems.at[count]
        )
        weight_copies = [
            pltpu.make_async_copy(weights[i], held.at[i], in_sems.at[i]) for i in range(count)
        ]
        state_copy.start()
        tile_copy.start()
        weight_copies[0].start()
        state_copy.wait()
        nodes[0, 0] = nodes[0, BLOCKS]
        tile_copy.wait()
        earlier = None
        for i in range(count):
            now = i % 2
            later = 1 - now
            weight_copies[i].wait()
            if i == 0:
                for j in range(1, count):
                    weight_copies[j].start()
            gain = held[i, 3 * D : 3 * D + GAIN_ROWS, :].astype(F32)
            gain = gain[0:1] + gain[1:2] + gain[2:3]
            for first in range(0, BLOCKS, CHUNK):
                sums = []
                for k in range(first, first + CHUNK):
                    both = jnp.concatenate(
                        [tiles[(k - 1) % BLOCKS, :, TILE:], tiles[k, :, :TILE]], axis=1
                    )
                    pair = nodes[now, k : k + 2].reshape(2 * TILE, D)
                    sums.append(jnp.dot(both, pair, preferred_element_type=F32).astype(BF))
                agg = jnp.concatenate(sums, axis=0)
                own = nodes[now, 1 + first : 1 + first + CHUNK].reshape(CHUNK * TILE, D)
                pre = jnp.dot(own, held[i, 0:D, :], preferred_element_type=F32)
                pre = pre + jnp.dot(agg, held[i, D : 2 * D, :], preferred_element_type=F32)
                hidden = jax.nn.silu(pre).astype(BF)
                if i == 0:
                    before = own.astype(F32)
                else:
                    before = trunk[first : first + CHUNK].reshape(CHUNK * TILE, D)
                value = before + jnp.dot(
                    hidden, held[i, 2 * D : 3 * D, :], preferred_element_type=F32
                )
                scale = lax.rsqrt(jnp.mean(value * value, axis=-1, keepdims=True) + 1e-06)
                updated = (value * scale * gain).reshape(CHUNK, TILE, D)
                if i < count - 1:
                    trunk[first : first + CHUNK] = updated
                new_nodes = updated.astype(BF)
                nodes[later, 1 + first : 1 + first + CHUNK] = new_nodes
                if first + CHUNK == BLOCKS and i < count - 1:
                    nodes[later, 0] = new_nodes[CHUNK - 1]
            copy = pltpu.make_async_copy(
                nodes.at[later, pl.ds(1, BLOCKS)], outs[i], out_sems.at[later]
            )
            copy.start()
            if earlier is not None:
                earlier.wait()
            earlier = copy
        earlier.wait()


def run_layers(t, flags, gathered, state, weights, outs):
    count = len(weights)
    kind_in = "gathered" if state is None else "bf16"
    states = [] if state is None else [state]
    where = pl.BlockSpec(memory_space=pltpu.HBM)
    n_in = 2 + len(states) + count
    return pl.pallas_call(
        functools.partial(layers_kernel, t, count, len(outs), kind_in),
        out_shape=[jax.ShapeDtypeStruct((BLOCKS, TILE, D), BF)] * count,
        in_specs=[pl.BlockSpec(memory_space=pltpu.SMEM)] + [where] * (n_in - 1 + len(outs)),
        out_specs=[where] * count,
        input_output_aliases={n_in + i: i for i in range(len(outs))},
        scratch_shapes=[
            pltpu.VMEM((count, 3 * D + GAIN_ROWS, D), BF),
            pltpu.VMEM((BLOCKS, TILE, 2 * TILE), BF),
            pltpu.VMEM((2, BLOCKS + 1, TILE, D), BF),
            pltpu.VMEM((BLOCKS, TILE, D), F32),
            pltpu.SemaphoreType.DMA((count + 2,)),
            pltpu.SemaphoreType.DMA((2,)),
        ],
        compiler_params=pltpu.CompilerParams(vmem_limit_bytes=62 << 20),
        cost_estimate=pl.CostEstimate(
            flops=count * 1_880_000_000, bytes_accessed=count * 4_000_000, transcendentals=0
        ),
    )(flags, gathered, *states, *weights, *outs)


def pick_kernel(flags, *refs):
    out = refs[-1]
    for i, source in enumerate(refs[:-1]):
        @pl.when(flags[PICK_AT] == i)
        def _():
            pltpu.sync_copy(source, out)


def pick(flags, sources):
    return pl.pallas_call(
        pick_kernel,
        out_shape=jax.ShapeDtypeStruct(sources[0].shape, sources[0].dtype),
        in_specs=[pl.BlockSpec(memory_space=pltpu.SMEM)]
        + [pl.BlockSpec(memory_space=pltpu.HBM)] * len(sources),
        out_specs=pl.BlockSpec(memory_space=pltpu.VMEM),
    )(flags, *sources)


def gain_as_rows(gain):
    high = lax.reduce_precision(gain, 8, 7)
    middle = lax.reduce_precision(gain - high, 8, 7)
    low = lax.reduce_precision(gain - high - middle, 8, 7)
    rows = jnp.stack([high, middle, low]).astype(BF)
    return jnp.pad(rows, ((0, GAIN_ROWS - 3), (0, 0)))


def on_device(node_feats, self_tiles, cross_tiles, cross_live, w_self, w_nbr, w_out, norm_gain):
    here = lax.axis_index("segment") * BLOCKS + lax.axis_index("node")
    flags = lax.dynamic_slice_in_dim(jnp.asarray(flag_table()), here, 1)[0]
    member = flags[MEMBER_AT]

    packed = jnp.concatenate([w_self[0], w_nbr[0], w_out[0], gain_as_rows(norm_gain[0])], axis=0)
    weights = [None] * len(STAGES)
    for supply in SUPPLIES:
        sent = [lax.ppermute(packed, AXES, weight_route(s, supply)) for s in range(slots_of(supply))]
        for t in supply:
            weights[t] = sent

    live = cross_live[member].astype(BF)[:, :, None]
    sent = jnp.concatenate(
        [node_feats[member], self_tiles[member], cross_tiles[member] * live], axis=-1
    )
    sent = jnp.broadcast_to(sent[:, None], (4, 2) + sent.shape[1:]).reshape((8,) + sent.shape[1:])
    gathered = lax.all_to_all(sent, "node", 0, 0, tiled=True)

    arrived = []
    state = None
    for release in RELEASES:
        outs = [None] * slots_of(release)
        for t in release:
            slot = 0
            for group in STAGES[t][1]:
                slots = range(slot, slot + len(group))
                old = [outs[s] for s in slots if outs[s] is not None]
                new = run_layers(
                    t, flags, gathered, state, [weights[t][s] for s in slots], old
                )
                for s, out in zip(slots, new):
                    outs[s] = out
                slot += len(group)
                state = new[-1]
            if t < len(STAGES) - 1:
                state = lax.ppermute(state, AXES, stage_route(t))
        arrived += [lax.ppermute(out, AXES, result_route(s, release)) for s, out in enumerate(outs)]

    home = pick(flags, arrived)
    spread = lax.all_to_all(home, "node", 0, 0, tiled=True)
    return spread.reshape(1, 4, 2, TILE, D)[:, :, 0]


def solution(mesh):
    return jax.shard_map(
        on_device,
        mesh=mesh,
        in_specs=(
            P(None, None, "node", None),
            P(None, None, "node", None),
            P(None, None, "node", None),
            P(None, None, "node"),
            P("segment", None, None),
            P("segment", None, None),
            P("segment", None, None),
            P("segment", None),
        ),
        out_specs=P("segment", None, "node", None),
        check_vma=False,
    )
```

```python
import functools

import jax
import jax.numpy as jnp
import numpy as np
from jax import lax
from jax.experimental import pallas as pl
from jax.experimental.pallas import tpu as pltpu
from jax.sharding import PartitionSpec as P

BF = jnp.bfloat16
F32 = jnp.float32
D = 512
TILE = 128
BLOCKS = 8
CHUNK = 4
MEMBERS = 4
AXES = ("segment", "node")
GAIN_ROWS = 16

STAGES = (
    (((0, 11), (0, 2), (0, 5), (0, 13)), ((0, 1), (2, 3))),
    (((2, 11), (2, 3), (1, 5), (1, 13)), ((4, 5, 6, 7, 8, 9),)),
    (((0, 10), (0, 3), (3, 5), (3, 13)), ((10, 11, 12, 13), (14, 15))),
)
SUPPLIES = ((0, 1, 2),)
RELEASES = ((0, 1, 2),)


def layers_of(t):
    return [layer for group in STAGES[t][1] for layer in group]


SLOTS = max(len(layers_of(t)) for t in range(len(STAGES)))
DEVICES = 512


def device(x, z, y, c):
    return (x * 16 + z) * BLOCKS + y * 2 + c


def over_chains(fn):
    pairs = [fn(m, y) for m in range(MEMBERS) for y in range(4)]
    return [(source, target) for source, target in pairs if source != target]


def chain(t, m, y):
    x, z = STAGES[t][0][m]
    return device(x, z, y, 1)


def home_of(layer, m, y):
    return device(layer // 4, layer % 4 * 4 + m, y, 0)


def weight_route(slot, supply):
    route = []
    for t in supply:
        if slot < len(layers_of(t)):
            layer = layers_of(t)[slot]
            route += over_chains(lambda m, y: (home_of(layer, m, y), chain(t, m, y)))
    return route


def slots_of(stages):
    return max(len(layers_of(t)) for t in stages)


def result_route(slot, release):
    route = []
    for t in release:
        if slot < len(layers_of(t)):
            layer = layers_of(t)[slot]
            route += over_chains(lambda m, y: (chain(t, m, y), home_of(layer, m, y)))
    return route


def stage_route(t):
    return over_chains(lambda m, y: (chain(t, m, y), chain(t + 1, m, y)))


PICK_AT = len(STAGES)
MEMBER_AT = PICK_AT + 1


def flag_table():
    table = np.zeros((DEVICES, MEMBER_AT + 1), np.int32)
    offset = 0
    for release in RELEASES:
        for t in release:
            for m in range(MEMBERS):
                for y in range(4):
                    at = chain(t, m, y)
                    table[at - 1 : at + 1, MEMBER_AT] = m
                    table[at, t] = 1
                    for slot, layer in enumerate(layers_of(t)):
                        table[home_of(layer, m, y), PICK_AT] = offset + slot
        offset += slots_of(release)
    return table


def layers_kernel(t, count, aliased, kind_in, *refs):
    flags, gathered = refs[:2]
    at = 2
    states = refs[at : at + (0 if kind_in == "gathered" else 1)]
    at += len(states)
    weights = refs[at : at + count]
    at += count + aliased
    outs = refs[at : at + count]
    held, tiles, nodes, trunk, in_sems, out_sems = refs[at + count :]

    @pl.when(flags[t] == 1)
    def _():
        source = gathered.at[:, :, pl.ds(0, D)] if kind_in == "gathered" else states[0]
        state_copy = pltpu.make_async_copy(
            source, nodes.at[0, pl.ds(1, BLOCKS)], in_sems.at[count + 1]
        )
        tile_copy = pltpu.make_async_copy(
            gathered.at[:, :, pl.ds(D, 2 * TILE)], tiles, in_sems.at[count]
        )
        weight_copies = [
            pltpu.make_async_copy(weights[i], held.at[i], in_sems.at[i]) for i in range(count)
        ]
        state_copy.start()
        tile_copy.start()
        weight_copies[0].start()
        state_copy.wait()
        nodes[0, 0] = nodes[0, BLOCKS]
        tile_copy.wait()
        earlier = None
        for i in range(count):
            now = i % 2
            later = 1 - now
            weight_copies[i].wait()
            if i == 0:
                for j in range(1, count):
                    weight_copies[j].start()
            gain = held[i, 3 * D : 3 * D + GAIN_ROWS, :].astype(F32)
            gain = gain[0:1] + gain[1:2] + gain[2:3]
            for first in range(0, BLOCKS, CHUNK):
                sums = []
                for k in range(first, first + CHUNK):
                    both = jnp.concatenate(
                        [tiles[(k - 1) % BLOCKS, :, TILE:], tiles[k, :, :TILE]], axis=1
                    )
                    pair = nodes[now, k : k + 2].reshape(2 * TILE, D)
                    sums.append(jnp.dot(both, pair, preferred_element_type=F32).astype(BF))
                agg = jnp.concatenate(sums, axis=0)
                own = nodes[now, 1 + first : 1 + first + CHUNK].reshape(CHUNK * TILE, D)
                pre = jnp.dot(own, held[i, 0:D, :], preferred_element_type=F32)
                pre = pre + jnp.dot(agg, held[i, D : 2 * D, :], preferred_element_type=F32)
                hidden = jax.nn.silu(pre).astype(BF)
                if i == 0:
                    before = own.astype(F32)
                else:
                    before = trunk[first : first + CHUNK].reshape(CHUNK * TILE, D)
                value = before + jnp.dot(
                    hidden, held[i, 2 * D : 3 * D, :], preferred_element_type=F32
                )
                scale = lax.rsqrt(jnp.mean(value * value, axis=-1, keepdims=True) + 1e-06)
                updated = (value * scale * gain).reshape(CHUNK, TILE, D)
                if i < count - 1:
                    trunk[first : first + CHUNK] = updated
                new_nodes = updated.astype(BF)
                nodes[later, 1 + first : 1 + first + CHUNK] = new_nodes
                if first + CHUNK == BLOCKS and i < count - 1:
                    nodes[later, 0] = new_nodes[CHUNK - 1]
            copy = pltpu.make_async_copy(
                nodes.at[later, pl.ds(1, BLOCKS)], outs[i], out_sems.at[later]
            )
            copy.start()
            if earlier is not None:
                earlier.wait()
            earlier = copy
        earlier.wait()


def run_layers(t, flags, gathered, state, weights, outs):
    count = len(weights)
    kind_in = "gathered" if state is None else "bf16"
    states = [] if state is None else [state]
    where = pl.BlockSpec(memory_space=pltpu.HBM)
    n_in = 2 + len(states) + count
    return pl.pallas_call(
        functools.partial(layers_kernel, t, count, len(outs), kind_in),
        out_shape=[jax.ShapeDtypeStruct((BLOCKS, TILE, D), BF)] * count,
        in_specs=[pl.BlockSpec(memory_space=pltpu.SMEM)] + [where] * (n_in - 1 + len(outs)),
        out_specs=[where] * count,
        input_output_aliases={n_in + i: i for i in range(len(outs))},
        scratch_shapes=[
            pltpu.VMEM((count, 3 * D + GAIN_ROWS, D), BF),
            pltpu.VMEM((BLOCKS, TILE, 2 * TILE), BF),
            pltpu.VMEM((2, BLOCKS + 1, TILE, D), BF),
            pltpu.VMEM((BLOCKS, TILE, D), F32),
            pltpu.SemaphoreType.DMA((count + 2,)),
            pltpu.SemaphoreType.DMA((2,)),
        ],
        compiler_params=pltpu.CompilerParams(vmem_limit_bytes=62 << 20),
        cost_estimate=pl.CostEstimate(
            flops=count * 1_880_000_000, bytes_accessed=count * 4_000_000, transcendentals=0
        ),
    )(flags, gathered, *states, *weights, *outs)


def pick_kernel(flags, *refs):
    out = refs[-1]
    for i, source in enumerate(refs[:-1]):
        @pl.when(flags[PICK_AT] == i)
        def _():
            pltpu.sync_copy(source, out)


def pick(flags, sources):
    return pl.pallas_call(
        pick_kernel,
        out_shape=jax.ShapeDtypeStruct(sources[0].shape, sources[0].dtype),
        in_specs=[pl.BlockSpec(memory_space=pltpu.SMEM)]
        + [pl.BlockSpec(memory_space=pltpu.HBM)] * len(sources),
        out_specs=pl.BlockSpec(memory_space=pltpu.VMEM),
    )(flags, *sources)


def gain_as_rows(gain):
    high = lax.reduce_precision(gain, 8, 7)
    middle = lax.reduce_precision(gain - high, 8, 7)
    low = lax.reduce_precision(gain - high - middle, 8, 7)
    rows = jnp.stack([high, middle, low]).astype(BF)
    return jnp.pad(rows, ((0, GAIN_ROWS - 3), (0, 0)))


def on_device(node_feats, self_tiles, cross_tiles, cross_live, w_self, w_nbr, w_out, norm_gain):
    here = lax.axis_index("segment") * BLOCKS + lax.axis_index("node")
    flags = lax.dynamic_slice_in_dim(jnp.asarray(flag_table()), here, 1)[0]
    member = flags[MEMBER_AT]

    packed = jnp.concatenate([w_self[0], w_nbr[0], w_out[0], gain_as_rows(norm_gain[0])], axis=0)
    weights = [None] * len(STAGES)
    for supply in SUPPLIES:
        sent = [lax.ppermute(packed, AXES, weight_route(s, supply)) for s in range(slots_of(supply))]
        for t in supply:
            weights[t] = sent

    live = cross_live[member].astype(BF)[:, :, None]
    sent = jnp.concatenate(
        [node_feats[member], self_tiles[member], cross_tiles[member] * live], axis=-1
    )
    sent = jnp.broadcast_to(sent[:, None], (4, 2) + sent.shape[1:]).reshape((8,) + sent.shape[1:])
    gathered = lax.all_to_all(sent, "node", 0, 0, tiled=True)

    arrived = []
    state = None
    for release in RELEASES:
        outs = [None] * slots_of(release)
        for t in release:
            slot = 0
            for group in STAGES[t][1]:
                slots = range(slot, slot + len(group))
                old = [outs[s] for s in slots if outs[s] is not None]
                new = run_layers(
                    t, flags, gathered, state, [weights[t][s] for s in slots], old
                )
                for s, out in zip(slots, new):
                    outs[s] = out
                slot += len(group)
                state = new[-1]
            if t < len(STAGES) - 1:
                state = lax.ppermute(state, AXES, stage_route(t))
        arrived += [lax.ppermute(out, AXES, result_route(s, release)) for s, out in enumerate(outs)]

    home = pick(flags, arrived)
    spread = lax.all_to_all(home, "node", 0, 0, tiled=True)
    return spread.reshape(1, 4, 2, TILE, D)[:, :, 0]


def solution(mesh):
    return jax.shard_map(
        on_device,
        mesh=mesh,
        in_specs=(
            P(None, None, "node", None),
            P(None, None, "node", None),
            P(None, None, "node", None),
            P(None, None, "node"),
            P("segment", None, None),
            P("segment", None, None),
            P("segment", None, None),
            P("segment", None),
        ),
        out_specs=P("segment", None, "node", None),
        check_vma=False,
    )
```

```python
import functools

import jax
import jax.numpy as jnp
import numpy as np
from jax import lax
from jax.experimental import pallas as pl
from jax.experimental.pallas import tpu as pltpu
from jax.sharding import PartitionSpec as P

BF = jnp.bfloat16
F32 = jnp.float32
D = 512
TILE = 128
BLOCKS = 8
CHUNK = 4
MEMBERS = 4
AXES = ("segment", "node")
GAIN_ROWS = 16

STAGES = (
    (((0, 15), (0, 6), (0, 9), (0, 1)), ((0, 1), (2, 3, 4))),
    (((2, 15), (2, 6), (1, 9), (1, 1)), ((5, 6, 7, 8, 9, 10),)),
    (((3, 15), (3, 6), (2, 9), (2, 1)), ((11, 12, 13), (14, 15))),
)
SUPPLIES = ((0, 1, 2),)
RELEASES = ((0, 1, 2),)


def layers_of(t):
    return [layer for group in STAGES[t][1] for layer in group]


SLOTS = max(len(layers_of(t)) for t in range(len(STAGES)))
DEVICES = 512


def device(x, z, y, c):
    return (x * 16 + z) * BLOCKS + y * 2 + c


def over_chains(fn):
    pairs = [fn(m, y) for m in range(MEMBERS) for y in range(4)]
    return [(source, target) for source, target in pairs if source != target]


def chain(t, m, y):
    x, z = STAGES[t][0][m]
    return device(x, z, y, 1)


def home_of(layer, m, y):
    return device(layer // 4, layer % 4 * 4 + m, y, 0)


def weight_route(slot, supply):
    route = []
    for t in supply:
        if slot < len(layers_of(t)):
            layer = layers_of(t)[slot]
            route += over_chains(lambda m, y: (home_of(layer, m, y), chain(t, m, y)))
    return route


def slots_of(stages):
    return max(len(layers_of(t)) for t in stages)


def result_route(slot, release):
    route = []
    for t in release:
        if slot < len(layers_of(t)):
            layer = layers_of(t)[slot]
            route += over_chains(lambda m, y: (chain(t, m, y), home_of(layer, m, y)))
    return route


def stage_route(t):
    return over_chains(lambda m, y: (chain(t, m, y), chain(t + 1, m, y)))


PICK_AT = len(STAGES)
MEMBER_AT = PICK_AT + 1


def flag_table():
    table = np.zeros((DEVICES, MEMBER_AT + 1), np.int32)
    offset = 0
    for release in RELEASES:
        for t in release:
            for m in range(MEMBERS):
                for y in range(4):
                    at = chain(t, m, y)
                    table[at - 1 : at + 1, MEMBER_AT] = m
                    table[at, t] = 1
                    for slot, layer in enumerate(layers_of(t)):
                        table[home_of(layer, m, y), PICK_AT] = offset + slot
        offset += slots_of(release)
    return table


def layers_kernel(t, count, aliased, kind_in, *refs):
    flags, gathered = refs[:2]
    at = 2
    states = refs[at : at + (0 if kind_in == "gathered" else 1)]
    at += len(states)
    weights = refs[at : at + count]
    at += count + aliased
    outs = refs[at : at + count]
    held, tiles, nodes, trunk, in_sems, out_sems = refs[at + count :]

    @pl.when(flags[t] == 1)
    def _():
        source = gathered.at[:, :, pl.ds(0, D)] if kind_in == "gathered" else states[0]
        state_copy = pltpu.make_async_copy(
            source, nodes.at[0, pl.ds(1, BLOCKS)], in_sems.at[count + 1]
        )
        tile_copy = pltpu.make_async_copy(
            gathered.at[:, :, pl.ds(D, 2 * TILE)], tiles, in_sems.at[count]
        )
        weight_copies = [
            pltpu.make_async_copy(weights[i], held.at[i], in_sems.at[i]) for i in range(count)
        ]
        state_copy.start()
        tile_copy.start()
        weight_copies[0].start()
        state_copy.wait()
        nodes[0, 0] = nodes[0, BLOCKS]
        tile_copy.wait()
        earlier = None
        for i in range(count):
            now = i % 2
            later = 1 - now
            weight_copies[i].wait()
            if i == 0:
                for j in range(1, count):
                    weight_copies[j].start()
            gain = held[i, 3 * D : 3 * D + GAIN_ROWS, :].astype(F32)
            gain = gain[0:1] + gain[1:2] + gain[2:3]
            for first in range(0, BLOCKS, CHUNK):
                sums = []
                for k in range(first, first + CHUNK):
                    both = jnp.concatenate(
                        [tiles[(k - 1) % BLOCKS, :, TILE:], tiles[k, :, :TILE]], axis=1
                    )
                    pair = nodes[now, k : k + 2].reshape(2 * TILE, D)
                    sums.append(jnp.dot(both, pair, preferred_element_type=F32).astype(BF))
                agg = jnp.concatenate(sums, axis=0)
                own = nodes[now, 1 + first : 1 + first + CHUNK].reshape(CHUNK * TILE, D)
                pre = jnp.dot(own, held[i, 0:D, :], preferred_element_type=F32)
                pre = pre + jnp.dot(agg, held[i, D : 2 * D, :], preferred_element_type=F32)
                hidden = jax.nn.silu(pre).astype(BF)
                if i == 0:
                    before = own.astype(F32)
                else:
                    before = trunk[first : first + CHUNK].reshape(CHUNK * TILE, D)
                value = before + jnp.dot(
                    hidden, held[i, 2 * D : 3 * D, :], preferred_element_type=F32
                )
                scale = lax.rsqrt(jnp.mean(value * value, axis=-1, keepdims=True) + 1e-06)
                updated = (value * scale * gain).reshape(CHUNK, TILE, D)
                if i < count - 1:
                    trunk[first : first + CHUNK] = updated
                new_nodes = updated.astype(BF)
                nodes[later, 1 + first : 1 + first + CHUNK] = new_nodes
                if first + CHUNK == BLOCKS and i < count - 1:
                    nodes[later, 0] = new_nodes[CHUNK - 1]
            copy = pltpu.make_async_copy(
                nodes.at[later, pl.ds(1, BLOCKS)], outs[i], out_sems.at[later]
            )
            copy.start()
            if earlier is not None:
                earlier.wait()
            earlier = copy
        earlier.wait()


def run_layers(t, flags, gathered, state, weights, outs):
    count = len(weights)
    kind_in = "gathered" if state is None else "bf16"
    states = [] if state is None else [state]
    where = pl.BlockSpec(memory_space=pltpu.HBM)
    n_in = 2 + len(states) + count
    return pl.pallas_call(
        functools.partial(layers_kernel, t, count, len(outs), kind_in),
        out_shape=[jax.ShapeDtypeStruct((BLOCKS, TILE, D), BF)] * count,
        in_specs=[pl.BlockSpec(memory_space=pltpu.SMEM)] + [where] * (n_in - 1 + len(outs)),
        out_specs=[where] * count,
        input_output_aliases={n_in + i: i for i in range(len(outs))},
        scratch_shapes=[
            pltpu.VMEM((count, 3 * D + GAIN_ROWS, D), BF),
            pltpu.VMEM((BLOCKS, TILE, 2 * TILE), BF),
            pltpu.VMEM((2, BLOCKS + 1, TILE, D), BF),
            pltpu.VMEM((BLOCKS, TILE, D), F32),
            pltpu.SemaphoreType.DMA((count + 2,)),
            pltpu.SemaphoreType.DMA((2,)),
        ],
        compiler_params=pltpu.CompilerParams(vmem_limit_bytes=62 << 20),
        cost_estimate=pl.CostEstimate(
            flops=count * 1_880_000_000, bytes_accessed=count * 4_000_000, transcendentals=0
        ),
    )(flags, gathered, *states, *weights, *outs)


def pick_kernel(flags, *refs):
    out = refs[-1]
    for i, source in enumerate(refs[:-1]):
        @pl.when(flags[PICK_AT] == i)
        def _():
            pltpu.sync_copy(source, out)


def pick(flags, sources):
    return pl.pallas_call(
        pick_kernel,
        out_shape=jax.ShapeDtypeStruct(sources[0].shape, sources[0].dtype),
        in_specs=[pl.BlockSpec(memory_space=pltpu.SMEM)]
        + [pl.BlockSpec(memory_space=pltpu.HBM)] * len(sources),
        out_specs=pl.BlockSpec(memory_space=pltpu.VMEM),
    )(flags, *sources)


def gain_as_rows(gain):
    high = lax.reduce_precision(gain, 8, 7)
    middle = lax.reduce_precision(gain - high, 8, 7)
    low = lax.reduce_precision(gain - high - middle, 8, 7)
    rows = jnp.stack([high, middle, low]).astype(BF)
    return jnp.pad(rows, ((0, GAIN_ROWS - 3), (0, 0)))


def on_device(node_feats, self_tiles, cross_tiles, cross_live, w_self, w_nbr, w_out, norm_gain):
    here = lax.axis_index("segment") * BLOCKS + lax.axis_index("node")
    flags = lax.dynamic_slice_in_dim(jnp.asarray(flag_table()), here, 1)[0]
    member = flags[MEMBER_AT]

    packed = jnp.concatenate([w_self[0], w_nbr[0], w_out[0], gain_as_rows(norm_gain[0])], axis=0)
    weights = [None] * len(STAGES)
    for supply in SUPPLIES:
        sent = [lax.ppermute(packed, AXES, weight_route(s, supply)) for s in range(slots_of(supply))]
        for t in supply:
            weights[t] = sent

    live = cross_live[member].astype(BF)[:, :, None]
    sent = jnp.concatenate(
        [node_feats[member], self_tiles[member], cross_tiles[member] * live], axis=-1
    )
    sent = jnp.broadcast_to(sent[:, None], (4, 2) + sent.shape[1:]).reshape((8,) + sent.shape[1:])
    gathered = lax.all_to_all(sent, "node", 0, 0, tiled=True)

    arrived = []
    state = None
    for release in RELEASES:
        outs = [None] * slots_of(release)
        for t in release:
            slot = 0
            for group in STAGES[t][1]:
                slots = range(slot, slot + len(group))
                old = [outs[s] for s in slots if outs[s] is not None]
                new = run_layers(
                    t, flags, gathered, state, [weights[t][s] for s in slots], old
                )
                for s, out in zip(slots, new):
                    outs[s] = out
                slot += len(group)
                state = new[-1]
            if t < len(STAGES) - 1:
                state = lax.ppermute(state, AXES, stage_route(t))
        arrived += [lax.ppermute(out, AXES, result_route(s, release)) for s, out in enumerate(outs)]

    home = pick(flags, arrived)
    spread = lax.all_to_all(home, "node", 0, 0, tiled=True)
    return spread.reshape(1, 4, 2, TILE, D)[:, :, 0]


def solution(mesh):
    return jax.shard_map(
        on_device,
        mesh=mesh,
        in_specs=(
            P(None, None, "node", None),
            P(None, None, "node", None),
            P(None, None, "node", None),
            P(None, None, "node"),
            P("segment", None, None),
            P("segment", None, None),
            P("segment", None, None),
            P("segment", None),
        ),
        out_specs=P("segment", None, "node", None),
        check_vma=False,
    )
```

```python
import functools

import jax
import jax.numpy as jnp
import numpy as np
from jax import lax
from jax.experimental import pallas as pl
from jax.experimental.pallas import tpu as pltpu
from jax.sharding import PartitionSpec as P

BF = jnp.bfloat16
F32 = jnp.float32
D = 512
TILE = 128
BLOCKS = 8
CHUNK = 4
MEMBERS = 4
AXES = ("segment", "node")
GAIN_ROWS = 16

STAGES = (
    (((0, 6), (0, 14), (0, 10), (0, 2)), ((0, 1), (2, 3, 4))),
    (((2, 6), (2, 14), (2, 10), (2, 2)), ((5, 6, 7, 8, 9, 10),)),
    (((3, 6), (3, 14), (1, 10), (1, 2)), ((11, 12), (13, 14, 15))),
)
SUPPLIES = ((0, 1, 2),)
RELEASES = ((0, 1, 2),)


def layers_of(t):
    return [layer for group in STAGES[t][1] for layer in group]


SLOTS = max(len(layers_of(t)) for t in range(len(STAGES)))
DEVICES = 512


def device(x, z, y, c):
    return (x * 16 + z) * BLOCKS + y * 2 + c


def over_chains(fn):
    pairs = [fn(m, y) for m in range(MEMBERS) for y in range(4)]
    return [(source, target) for source, target in pairs if source != target]


def chain(t, m, y):
    x, z = STAGES[t][0][m]
    return device(x, z, y, 1)


def home_of(layer, m, y):
    return device(layer // 4, layer % 4 * 4 + m, y, 0)


def weight_route(slot, supply):
    route = []
    for t in supply:
        if slot < len(layers_of(t)):
            layer = layers_of(t)[slot]
            route += over_chains(lambda m, y: (home_of(layer, m, y), chain(t, m, y)))
    return route


def slots_of(stages):
    return max(len(layers_of(t)) for t in stages)


def result_route(slot, release):
    route = []
    for t in release:
        if slot < len(layers_of(t)):
            layer = layers_of(t)[slot]
            route += over_chains(lambda m, y: (chain(t, m, y), home_of(layer, m, y)))
    return route


def stage_route(t):
    return over_chains(lambda m, y: (chain(t, m, y), chain(t + 1, m, y)))


PICK_AT = len(STAGES)
MEMBER_AT = PICK_AT + 1


def flag_table():
    table = np.zeros((DEVICES, MEMBER_AT + 1), np.int32)
    offset = 0
    for release in RELEASES:
        for t in release:
            for m in range(MEMBERS):
                for y in range(4):
                    at = chain(t, m, y)
                    table[at - 1 : at + 1, MEMBER_AT] = m
                    table[at, t] = 1
                    for slot, layer in enumerate(layers_of(t)):
                        table[home_of(layer, m, y), PICK_AT] = offset + slot
        offset += slots_of(release)
    return table


def layers_kernel(t, count, aliased, kind_in, *refs):
    flags, gathered = refs[:2]
    at = 2
    states = refs[at : at + (0 if kind_in == "gathered" else 1)]
    at += len(states)
    weights = refs[at : at + count]
    at += count + aliased
    outs = refs[at : at + count]
    held, tiles, nodes, trunk, in_sems, out_sems = refs[at + count :]

    @pl.when(flags[t] == 1)
    def _():
        source = gathered.at[:, :, pl.ds(0, D)] if kind_in == "gathered" else states[0]
        state_copy = pltpu.make_async_copy(
            source, nodes.at[0, pl.ds(1, BLOCKS)], in_sems.at[count + 1]
        )
        tile_copy = pltpu.make_async_copy(
            gathered.at[:, :, pl.ds(D, 2 * TILE)], tiles, in_sems.at[count]
        )
        weight_copies = [
            pltpu.make_async_copy(weights[i], held.at[i], in_sems.at[i]) for i in range(count)
        ]
        state_copy.start()
        tile_copy.start()
        weight_copies[0].start()
        state_copy.wait()
        nodes[0, 0] = nodes[0, BLOCKS]
        tile_copy.wait()
        earlier = None
        for i in range(count):
            now = i % 2
            later = 1 - now
            weight_copies[i].wait()
            if i == 0:
                for j in range(1, count):
                    weight_copies[j].start()
            gain = held[i, 3 * D : 3 * D + GAIN_ROWS, :].astype(F32)
            gain = gain[0:1] + gain[1:2] + gain[2:3]
            for first in range(0, BLOCKS, CHUNK):
                sums = []
                for k in range(first, first + CHUNK):
                    both = jnp.concatenate(
                        [tiles[(k - 1) % BLOCKS, :, TILE:], tiles[k, :, :TILE]], axis=1
                    )
                    pair = nodes[now, k : k + 2].reshape(2 * TILE, D)
                    sums.append(jnp.dot(both, pair, preferred_element_type=F32).astype(BF))
                agg = jnp.concatenate(sums, axis=0)
                own = nodes[now, 1 + first : 1 + first + CHUNK].reshape(CHUNK * TILE, D)
                pre = jnp.dot(own, held[i, 0:D, :], preferred_element_type=F32)
                pre = pre + jnp.dot(agg, held[i, D : 2 * D, :], preferred_element_type=F32)
                hidden = jax.nn.silu(pre).astype(BF)
                if i == 0:
                    before = own.astype(F32)
                else:
                    before = trunk[first : first + CHUNK].reshape(CHUNK * TILE, D)
                value = before + jnp.dot(
                    hidden, held[i, 2 * D : 3 * D, :], preferred_element_type=F32
                )
                scale = lax.rsqrt(jnp.mean(value * value, axis=-1, keepdims=True) + 1e-06)
                updated = (value * scale * gain).reshape(CHUNK, TILE, D)
                if i < count - 1:
                    trunk[first : first + CHUNK] = updated
                new_nodes = updated.astype(BF)
                nodes[later, 1 + first : 1 + first + CHUNK] = new_nodes
                if first + CHUNK == BLOCKS and i < count - 1:
                    nodes[later, 0] = new_nodes[CHUNK - 1]
            copy = pltpu.make_async_copy(
                nodes.at[later, pl.ds(1, BLOCKS)], outs[i], out_sems.at[later]
            )
            copy.start()
            if earlier is not None:
                earlier.wait()
            earlier = copy
        earlier.wait()


def run_layers(t, flags, gathered, state, weights, outs):
    count = len(weights)
    kind_in = "gathered" if state is None else "bf16"
    states = [] if state is None else [state]
    where = pl.BlockSpec(memory_space=pltpu.HBM)
    n_in = 2 + len(states) + count
    return pl.pallas_call(
        functools.partial(layers_kernel, t, count, len(outs), kind_in),
        out_shape=[jax.ShapeDtypeStruct((BLOCKS, TILE, D), BF)] * count,
        in_specs=[pl.BlockSpec(memory_space=pltpu.SMEM)] + [where] * (n_in - 1 + len(outs)),
        out_specs=[where] * count,
        input_output_aliases={n_in + i: i for i in range(len(outs))},
        scratch_shapes=[
            pltpu.VMEM((count, 3 * D + GAIN_ROWS, D), BF),
            pltpu.VMEM((BLOCKS, TILE, 2 * TILE), BF),
            pltpu.VMEM((2, BLOCKS + 1, TILE, D), BF),
            pltpu.VMEM((BLOCKS, TILE, D), F32),
            pltpu.SemaphoreType.DMA((count + 2,)),
            pltpu.SemaphoreType.DMA((2,)),
        ],
        compiler_params=pltpu.CompilerParams(vmem_limit_bytes=62 << 20),
        cost_estimate=pl.CostEstimate(
            flops=count * 1_880_000_000, bytes_accessed=count * 4_000_000, transcendentals=0
        ),
    )(flags, gathered, *states, *weights, *outs)


def pick_kernel(flags, *refs):
    out = refs[-1]
    for i, source in enumerate(refs[:-1]):
        @pl.when(flags[PICK_AT] == i)
        def _():
            pltpu.sync_copy(source, out)


def pick(flags, sources):
    return pl.pallas_call(
        pick_kernel,
        out_shape=jax.ShapeDtypeStruct(sources[0].shape, sources[0].dtype),
        in_specs=[pl.BlockSpec(memory_space=pltpu.SMEM)]
        + [pl.BlockSpec(memory_space=pltpu.HBM)] * len(sources),
        out_specs=pl.BlockSpec(memory_space=pltpu.VMEM),
    )(flags, *sources)


def gain_as_rows(gain):
    high = lax.reduce_precision(gain, 8, 7)
    middle = lax.reduce_precision(gain - high, 8, 7)
    low = lax.reduce_precision(gain - high - middle, 8, 7)
    rows = jnp.stack([high, middle, low]).astype(BF)
    return jnp.pad(rows, ((0, GAIN_ROWS - 3), (0, 0)))


def on_device(node_feats, self_tiles, cross_tiles, cross_live, w_self, w_nbr, w_out, norm_gain):
    here = lax.axis_index("segment") * BLOCKS + lax.axis_index("node")
    flags = lax.dynamic_slice_in_dim(jnp.asarray(flag_table()), here, 1)[0]
    member = flags[MEMBER_AT]

    packed = jnp.concatenate([w_self[0], w_nbr[0], w_out[0], gain_as_rows(norm_gain[0])], axis=0)
    weights = [None] * len(STAGES)
    for supply in SUPPLIES:
        sent = [lax.ppermute(packed, AXES, weight_route(s, supply)) for s in range(slots_of(supply))]
        for t in supply:
            weights[t] = sent

    live = cross_live[member].astype(BF)[:, :, None]
    sent = jnp.concatenate(
        [node_feats[member], self_tiles[member], cross_tiles[member] * live], axis=-1
    )
    sent = jnp.broadcast_to(sent[:, None], (4, 2) + sent.shape[1:]).reshape((8,) + sent.shape[1:])
    gathered = lax.all_to_all(sent, "node", 0, 0, tiled=True)

    arrived = []
    state = None
    for release in RELEASES:
        outs = [None] * slots_of(release)
        for t in release:
            slot = 0
            for group in STAGES[t][1]:
                slots = range(slot, slot + len(group))
                old = [outs[s] for s in slots if outs[s] is not None]
                new = run_layers(
                    t, flags, gathered, state, [weights[t][s] for s in slots], old
                )
                for s, out in zip(slots, new):
                    outs[s] = out
                slot += len(group)
                state = new[-1]
            if t < len(STAGES) - 1:
                state = lax.ppermute(state, AXES, stage_route(t))
        arrived += [lax.ppermute(out, AXES, result_route(s, release)) for s, out in enumerate(outs)]

    home = pick(flags, arrived)
    spread = lax.all_to_all(home, "node", 0, 0, tiled=True)
    return spread.reshape(1, 4, 2, TILE, D)[:, :, 0]


def solution(mesh):
    return jax.shard_map(
        on_device,
        mesh=mesh,
        in_specs=(
            P(None, None, "node", None),
            P(None, None, "node", None),
            P(None, None, "node", None),
            P(None, None, "node"),
            P("segment", None, None),
            P("segment", None, None),
            P("segment", None, None),
            P("segment", None),
        ),
        out_specs=P("segment", None, "node", None),
        check_vma=False,
    )
```
